128 devices in a mesh: row: 8 (over z, y_lo), col: 16 (over y_hi, x, core).
Axes of the slice: x: 4, y: 4 (y_hi: 2, y_lo: 2; y = y_hi * 2 + y_lo), z: 4, core: 2. Of those that a mesh axis runs over, the one named last changes fastest.
Arguments:
- blocks: float32 [8, 16, 170, 128, 128], P('row', 'col'), may hold values from -1 to 1
- coords: int32 [8, 16, 2, 170], P('row', 'col'), may hold values from 0 to 31, as said below
- vectors: float32 [2, 32768, 128], P(None, ('row', 'col')), may hold values from -6 to 6
Outputs:
- basis: float32 [2, 32768, 128], P(None, ('row', 'col'))
The draws below stay inside these ranges and needn't reach their ends.
Inputs may be any that keep to these rules, and one draw needn't show every extreme that they name: Within each tile the 170 listed positions are distinct, and the positions (0, 0) and (31, 15) are always listed; coords[r, c, 0, k] is below 32 and coords[r, c, 1, k] below 16.
All inputs are finite; a program needn't handle non-finite values.
Results may differ from the reference program's by a relative error of at most 0.0003.
Values sent between devices are 32-bit elements; how exact they have to be, the bound alone decides.
A program may use at most 192 MiB of HBM per device.

```python
import jax
import jax.numpy as jnp
from jax import lax

BLK = 128
NV = 128
TILE = 2048
APPS = 2
ORDER = 32768
ROWS = 4096
GROUP = 256
NBLK = 170
N_ROW = 8
N_COL = 16


def draw_blocks(key, part):
    shape_all = (N_ROW, N_COL, NBLK, BLK, BLK)
    entries = jax.random.uniform(key, shape_all, jnp.float32, -1.0, 1.0)
    return entries


def draw_coords(key, part):
    block_rows = ROWS // BLK
    block_cols = TILE // BLK
    total_spots = block_rows * block_cols
    key_list = jax.random.split(jax.random.fold_in(key, 5), N_ROW * N_COL)

    def one_tile(tile_key):
        middle = jax.random.permutation(tile_key, total_spots - 2)[:NBLK - 2].astype(jnp.int32) + 1
        chosen = jnp.concatenate([jnp.zeros((1,), jnp.int32), middle, jnp.full((1,), total_spots - 1, jnp.int32)])
        chosen = jax.random.permutation(jax.random.fold_in(tile_key, 3), chosen)
        return jnp.stack([chosen // block_cols, chosen % block_cols])
    return jax.vmap(one_tile)(key_list).reshape(N_ROW, N_COL, 2, NBLK).astype(jnp.int32)


def shard_levels(rng, shape, cuts, smallest, largest):
    gain = 1.0
    for dim, shards_of in cuts:
        draws = jax.random.uniform(jax.random.fold_in(jax.random.fold_in(rng, 6), dim), (shards_of,), jnp.float32, smallest / len(cuts), largest / len(cuts))
        gain = gain * jnp.repeat(jnp.exp(draws), shape[dim] // shards_of).reshape((-1,) + (1,) * (len(shape) - 1 - dim))
    return gain


def normal_values(key, dims, scale, most, pieces=(), kind=jnp.bfloat16):
    values = scale * jax.random.normal(key, dims, jnp.float32)
    if pieces:
        values = values * shard_levels(key, dims, pieces, -0.22, 0.18)
    return jnp.clip(values, -most, most).astype(kind)


def setup_inputs(seed: int = 0) -> dict:
    arg_keys = jax.random.split(jax.random.key(seed), 4)
    blocks = draw_blocks(jax.random.fold_in(arg_keys[3], 71), 0)
    coords = draw_coords(jax.random.fold_in(arg_keys[3], 71), 0)
    vectors = normal_values(arg_keys[2], (2, ORDER, NV), 1.0, 6.0, ((1, 128),), jnp.float32)
    return dict(blocks=blocks, coords=coords, vectors=vectors)


exact_mode = lax.Precision.HIGHEST

def tile_products(values, places, col_side, row_side):
    blk_size = values.shape[1]
    listed = values.shape[0]
    row_blocks = row_side.shape[0] // blk_size
    col_blocks = col_side.shape[0] // blk_size
    row_of = places[0]
    col_of = places[1]
    col_pieces = col_side.reshape(col_blocks, blk_size, -1)[col_of]
    direct = jnp.einsum('kab,kbv->kav', values, col_pieces, precision=exact_mode)
    row_pieces = row_side.reshape(row_blocks, blk_size, -1)[row_of]
    flipped = jnp.einsum('kba,kbv->kav', values, row_pieces, precision=exact_mode)
    row_hot = (row_of[None, :] == jnp.arange(row_blocks, dtype=jnp.int32)[:, None]).astype(values.dtype)
    col_hot = (col_of[None, :] == jnp.arange(col_blocks, dtype=jnp.int32)[:, None]).astype(values.dtype)
    out_rows = jnp.dot(row_hot, direct.reshape(listed, -1), precision=exact_mode).reshape(row_side.shape[0], -1)
    out_cols = jnp.dot(col_hot, flipped.reshape(listed, -1), precision=exact_mode).reshape(col_side.shape[0], -1)
    return (out_rows, out_cols)

def normal_basis(applied, factor):
    return lax.linalg.triangular_solve(factor, applied, left_side=False, lower=True, transpose_a=True)

def apply_full(upper, lower, blocks, coords):
    upper_grid = upper.reshape(N_ROW, N_COL, GROUP, NV)
    lower_grid = lower.reshape(N_ROW, N_COL, GROUP, NV)

    def visit_tile(carry, tile_item):
        sum_upper, sum_lower = carry
        values, places, flat_id = tile_item
        row_id = flat_id // N_COL
        col_id = flat_id % N_COL
        col_side = lax.dynamic_index_in_dim(lower_grid, col_id, 1, keepdims=False).reshape(TILE, NV)
        row_side = lax.dynamic_index_in_dim(upper_grid, row_id, 0, keepdims=False).reshape(ROWS, NV)
        out_rows, out_cols = tile_products(values, places, col_side, row_side)
        sum_upper = sum_upper.at[row_id].add(out_rows.reshape(N_COL, GROUP, NV))
        sum_lower = sum_lower.at[:, col_id].add(out_cols.reshape(N_ROW, GROUP, NV))
        return ((sum_upper, sum_lower), None)
    start_sum = jnp.zeros((N_ROW, N_COL, GROUP, NV), jnp.float32)
    flat_ids = jnp.arange(N_ROW * N_COL, dtype=jnp.int32)
    summed, unused = lax.scan(visit_tile, (start_sum, start_sum), (blocks.reshape(N_ROW * N_COL, NBLK, BLK, BLK), coords.reshape(N_ROW * N_COL, 2, NBLK), flat_ids))
    return (summed[0].reshape(ORDER, NV), summed[1].reshape(ORDER, NV))

def reference(blocks, coords, vectors):
    upper = vectors[0]
    lower = vectors[1]
    for app_index in range(APPS):
        new_upper, new_lower = apply_full(upper, lower, blocks, coords)
        gram_sum = (jnp.einsum('nv,nw->vw', new_upper, new_upper, precision=exact_mode) + jnp.einsum('nv,nw->vw', new_lower, new_lower, precision=exact_mode)) / (2 * ORDER)
        factor = jnp.linalg.cholesky(gram_sum)
        upper = normal_basis(new_upper, factor)
        lower = normal_basis(new_lower, factor)
    return jnp.stack([upper, lower])
```

```python
import functools

import jax
import jax.numpy as jnp
from jax import lax
from jax.experimental import pallas as pl
from jax.experimental.pallas import tpu as pltpu
from jax.sharding import PartitionSpec as P

MESH = pl.DeviceIdType.MESH
HIGH = lax.Precision.HIGHEST
F32 = jnp.float32
BF16 = jnp.bfloat16

GROUP = 256
NV = 128
BLK = 128
NROW = 8
NCOL = 16
CHUNK = 10
LIFT = 2.0**20


class Where:
    def __init__(self):
        self.r = lax.axis_index("row")
        self.c = lax.axis_index("col")
        self.z = self.r // 2
        self.yl = self.r % 2
        self.yh = self.c // 8
        self.x = (self.c // 2) % 4
        self.core = self.c % 2

    def zr(self, dz, other=False):
        yl = 1 - self.yl if other else self.yl
        return ((self.z + dz) % 4) * 2 + yl

    def xc(self, dx, other_y=False, other_core=False):
        yh = 1 - self.yh if other_y else self.yh
        core = 1 - self.core if other_core else self.core
        return (yh * 4 + (self.x + dx) % 4) * 2 + core

    def neighbours(self):
        out = [(self.zr(dz), self.c) for dz in (1, 2, 3)]
        out.append((self.zr(0, True), self.c))
        out += [(self.r, self.xc(dx)) for dx in (1, 2, 3)]
        out.append((self.r, self.xc(0, True)))
        out.append((self.r, self.xc(0, False, True)))
        return out

    def all_group(self):
        out = [((self.r + d) % NROW, self.c) for d in range(1, NROW)]
        out += [(self.r, (self.c + d) % NCOL) for d in range(1, NCOL)]
        return out


def entry_barrier(partners):
    barrier = pltpu.get_barrier_semaphore()
    for p in partners:
        pl.semaphore_signal(barrier, inc=1, device_id=p, device_id_type=MESH)
    pl.semaphore_wait(barrier, len(partners))


def rcopy(src, dst, send, recv, dev):
    return pltpu.make_async_remote_copy(
        src_ref=src,
        dst_ref=dst,
        send_sem=send,
        recv_sem=recv,
        device_id=dev,
        device_id_type=MESH,
    )


class Gather:
    def __init__(self, w, up, lo, rowbuf, colbuf, su, ru, sl, rl):
        self.w, self.up, self.lo = w, up, lo
        self.rowbuf, self.colbuf = rowbuf, colbuf
        self.su, self.ru, self.sl, self.rl = su, ru, sl, rl
        self.sent = []
        self.nu = 0
        self.nl = 0

    def send_u(self, src, piece, dev):
        cp = rcopy(src, self.rowbuf.at[piece], self.su.at[self.nu], self.ru.at[piece], dev)
        self.nu += 1
        cp.start()
        self.sent.append(cp)

    def send_l(self, src, piece, dev):
        cp = rcopy(src, self.colbuf.at[piece], self.sl.at[self.nl], self.rl.at[piece], dev)
        self.nl += 1
        cp.start()
        self.sent.append(cp)

    def wait_u(self, piece):
        ref = self.rowbuf.at[piece]
        rcopy(ref, ref, self.su.at[0], self.ru.at[piece], (self.w.r, self.w.xc(0, True))).wait_recv()

    def wait_l(self, piece):
        ref = self.colbuf.at[piece]
        rcopy(ref, ref, self.sl.at[0], self.rl.at[piece], (self.w.zr(0, True), self.w.c)).wait_recv()

    def start(self):
        w = self.w
        self.send_u(self.up, w.c, (w.r, w.xc(0, True)))
        self.send_l(self.lo, w.r, (w.zr(0, True), w.c))
        for d in (2, 1, 3):
            self.send_u(self.up, w.c, (w.r, w.xc(d)))
            self.send_l(self.lo, w.r, (w.zr(d), w.c))
        self.send_u(self.up, w.c, (w.r, w.xc(0, False, True)))
        self.rowbuf[w.c] = self.up[...]
        self.colbuf[w.r] = self.lo[...]

    def forward_y(self):
        w = self.w
        pu = w.xc(0, True)
        ql = w.zr(0, True)
        self.wait_l(ql)
        for d in (2, 1, 3):
            self.send_l(self.colbuf.at[ql], ql, (w.zr(d), w.c))
        self.wait_u(pu)
        for d in (2, 1, 3):
            self.send_u(self.rowbuf.at[pu], pu, (w.r, w.xc(d)))
        self.send_u(self.rowbuf.at[pu], pu, (w.r, w.xc(0, False, True)))

    def forward_x(self, other_y):
        w = self.w
        for d in (1, 3, 2):
            p = w.xc(d, other_y)
            self.wait_u(p)
            self.send_u(self.rowbuf.at[p], p, (w.r, w.xc(0, False, True)))

    def finish(self):
        w = self.w
        for other in (False, True):
            for d in (1, 2, 3):
                self.wait_l(w.zr(d, other))
        for other in (False, True):
            for d in (0, 1, 2, 3):
                self.wait_u(w.xc(d, other, True))
        for cp in self.sent:
            cp.wait_send()


def gather_kernel(vec, rowbuf, colbuf, su, ru, sl, rl):
    w = Where()
    entry_barrier(w.neighbours())
    g = Gather(w, vec.at[0], vec.at[1], rowbuf, colbuf, su, ru, sl, rl)
    g.start()
    g.forward_y()
    g.forward_x(False)
    g.forward_x(True)
    g.finish()


GATHER_SEMS = [
    pltpu.SemaphoreType.DMA((15,)),
    pltpu.SemaphoreType.DMA((16,)),
    pltpu.SemaphoreType.DMA((7,)),
    pltpu.SemaphoreType.DMA((8,)),
]


def reduce_scatter(w, rows, cols, acc, sib, xbuf, yhbuf, zbuf, ylbuf, mid, s_s, r_s, s_x, r_x, s_z, r_z, s_y, r_y, between=None):
    sent = []
    sibling = (w.r, w.xc(0, False, True))
    order = [(d, o) for d in (2, 1, 3, 0) for o in (True, False)]
    for i, (d, o) in enumerate(order):
        cp = rcopy(rows.at[w.xc(d, o, True)], sib.at[i], s_s.at[i], r_s.at[i], sibling)
        cp.start()
        sent.append(cp)
    for i, d in enumerate((2, 1, 3)):
        for j, o in enumerate((True, False)):
            cp = rcopy(cols.at[w.zr(d, o)], zbuf.at[i, j], s_z.at[i, j], r_z.at[i, j], (w.zr(d), w.c))
            cp.start()
            sent.append(cp)
    for i, (d, o) in enumerate(order):
        sent[i].wait_recv()
        acc[i] = rows[w.xc(d, o)] + sib[i]
        if d:
            k, j = i // 2, i % 2
            cp = rcopy(acc.at[i], xbuf.at[k, j], s_x.at[k, j], r_x.at[k, j], (w.r, w.xc(d)))
            cp.start()
            sent.append(cp)
    zc = [c for c in sent[8:14]]
    xc = [c for c in sent[14:20]]
    if between is not None:
        between()
    for i in range(3):
        zc[2 * i].wait_recv()
    mid[0] = cols[w.zr(0, True)] + zbuf[0, 0] + zbuf[1, 0] + zbuf[2, 0]
    cl = rcopy(mid.at[0], ylbuf, s_y.at[0], r_y.at[0], (w.zr(0, True), w.c))
    cl.start()
    for i in range(3):
        xc[2 * i].wait_recv()
    mid[1] = acc[6] + xbuf[0, 0] + xbuf[1, 0] + xbuf[2, 0]
    cu = rcopy(mid.at[1], yhbuf, s_y.at[1], r_y.at[1], (w.r, w.xc(0, True)))
    cu.start()
    for i in range(3):
        zc[2 * i + 1].wait_recv()
    lower = cols[w.zr(0)] + zbuf[0, 1] + zbuf[1, 1] + zbuf[2, 1]
    mid[2] = lower
    for i in range(3):
        xc[2 * i + 1].wait_recv()
    mid[3] = acc[7] + xbuf[0, 1] + xbuf[1, 1] + xbuf[2, 1]
    cl.wait_recv()
    lower = mid[2] + ylbuf[...]
    cu.wait_recv()
    upper = mid[3] + yhbuf[...]
    for cp in sent:
        cp.wait_send()
    cl.wait_send()
    cu.wait_send()
    return upper, lower


RS_SCRATCH = [
    pltpu.VMEM((8, GROUP, NV), F32),
    pltpu.VMEM((8, GROUP, NV), F32),
    pltpu.VMEM((3, 2, GROUP, NV), F32),
    pltpu.VMEM((GROUP, NV), F32),
    pltpu.VMEM((3, 2, GROUP, NV), F32),
    pltpu.VMEM((GROUP, NV), F32),
    pltpu.VMEM((4, GROUP, NV), F32),
    pltpu.SemaphoreType.DMA((8,)),
    pltpu.SemaphoreType.DMA((8,)),
    pltpu.SemaphoreType.DMA((3, 2)),
    pltpu.SemaphoreType.DMA((3, 2)),
    pltpu.SemaphoreType.DMA((3, 2)),
    pltpu.SemaphoreType.DMA((3, 2)),
    pltpu.SemaphoreType.DMA((2,)),
    pltpu.SemaphoreType.DMA((2,)),
]


class GramSum:
    def __init__(self, w, part, g1, s1, g2, s2, full, ss, rr):
        self.w, self.part, self.g1, self.s1, self.g2, self.s2, self.full = w, part, g1, s1, g2, s2, full
        self.ss, self.rr = ss, rr
        self.sent = []

    def exchange(self, lo, count, src_of, dst, me, dev_of):
        cps = []
        for d in range(1, count):
            cp = rcopy(src_of(d), dst.at[me], self.ss.at[lo + d], self.rr.at[lo + d], dev_of(d))
            cp.start()
            cps.append(cp)
        self.sent += cps
        return cps

    def phase1(self):
        w = self.w

        def src(d):
            return self.part.at[(w.c + d) % NCOL]

        self.cps = self.exchange(0, NCOL, src, self.g1, w.c, lambda d: (w.r, (w.c + d) % NCOL))
        self.g1[w.c] = self.part[w.c]

    def phase2(self):
        w = self.w
        for cp in self.cps:
            cp.wait_recv()
        total = self.g1[0]
        for i in range(1, NCOL):
            total = total + self.g1[i]
        self.s1[...] = total
        self.cps = self.exchange(NCOL, NROW, lambda d: self.s1, self.g2, w.r, lambda d: ((w.r + d) % NROW, w.c))
        self.g2[w.r] = total

    def phase3(self):
        w = self.w
        for cp in self.cps:
            cp.wait_recv()
        total = self.g2[0]
        for i in range(1, NROW):
            total = total + self.g2[i]
        total = total * (1.0 / (2 * GROUP * NROW * NCOL))
        self.s2[...] = total
        self.cps = self.exchange(
            NCOL + NROW, NCOL, lambda d: self.s2, self.full, w.c, lambda d: (w.r, (w.c + d) % NCOL)
        )
        self.full[w.c] = total

    def finish(self):
        for cp in self.cps:
            cp.wait_recv()
        for cp in self.sent:
            cp.wait_send()


GRAM_SCRATCH = [
    pltpu.VMEM((NCOL, 8, NV), F32),
    pltpu.VMEM((NCOL, 8, NV), F32),
    pltpu.VMEM((8, NV), F32),
    pltpu.VMEM((NROW, 8, NV), F32),
    pltpu.VMEM((8, NV), F32),
    pltpu.SemaphoreType.DMA((2 * NCOL + NROW,)),
    pltpu.SemaphoreType.DMA((2 * NCOL + NROW,)),
]


def self_product(v):
    return lax.dot_general(v, v, (((0,), (0,)), ((), ())), precision=HIGH, preferred_element_type=F32)


def middle_kernel(rows, cols, rowbuf, colbuf, gram, acc, sib, xbuf, yhbuf, zbuf, ylbuf, mid, s_s, r_s, s_x, r_x, s_z, r_z, s_y, r_y, both, su, ru, sl, rl, part, g1, s1, g2, s2, ss, rr):
    w = Where()
    entry_barrier(w.all_group())
    upper, lower = reduce_scatter(w, rows, cols, acc, sib, xbuf, yhbuf, zbuf, ylbuf, mid, s_s, r_s, s_x, r_x, s_z, r_z, s_y, r_y)
    both[0] = upper * LIFT
    both[1] = lower * LIFT
    g = Gather(w, both.at[0], both.at[1], rowbuf, colbuf, su, ru, sl, rl)
    g.start()
    part[...] = (self_product(both[0]) + self_product(both[1])).reshape(NCOL, 8, NV)
    s = GramSum(w, part, g1, s1, g2, s2, gram, ss, rr)
    s.phase1()
    g.forward_y()
    s.phase2()
    g.forward_x(False)
    s.phase3()
    g.forward_x(True)
    g.finish()
    s.finish()


def times_inverse(v, linv):
    return lax.dot_general(v, linv, (((1,), (1,)), ((), ())), precision=HIGH, preferred_element_type=F32)


def last_kernel(rows, cols, linv, out, gram, acc, sib, xbuf, yhbuf, zbuf, ylbuf, mid, s_s, r_s, s_x, r_x, s_z, r_z, s_y, r_y, part, g1, s1, g2, s2, ss, rr):
    w = Where()
    entry_barrier(w.all_group())
    upper, lower = reduce_scatter(w, rows, cols, acc, sib, xbuf, yhbuf, zbuf, ylbuf, mid, s_s, r_s, s_x, r_x, s_z, r_z, s_y, r_y)
    out[0] = times_inverse(upper, linv[...])
    out[1] = times_inverse(lower, linv[...])
    part[...] = (self_product(out[0]) + self_product(out[1])).reshape(NCOL, 8, NV)
    s = GramSum(w, part, g1, s1, g2, s2, gram, ss, rr)
    s.phase1()
    s.phase2()
    s.phase3()
    s.finish()


def inverse_factor(gram):
    tiles = [gram[t * 8 : t * 8 + 8, :] for t in range(16)]
    lane = lax.broadcasted_iota(jnp.int32, (8, NV), 1)
    sub = lax.broadcasted_iota(jnp.int32, (8, NV), 0)
    for j in range(NV):
        t0, i0 = j // 8, j % 8
        here = lane == j
        row = tiles[t0][i0 : i0 + 1, :]
        inv = 1.0 / row[:, j : j + 1]
        step = jnp.where(here[0:1], 1.0, row) * inv
        for t in range(t0, 16):
            tile = tiles[t]
            col = jnp.broadcast_to(tile[:, j : j + 1], (8, NV))
            new = jnp.where(here, 0.0, tile) - col * step
            tiles[t] = jnp.where(sub > i0, new, tile) if t == t0 else new
    out = []
    for t in range(16):
        tile = tiles[t]
        diag = jnp.sum(jnp.where(lane == sub + 8 * t, tile, 0.0), axis=1, keepdims=True)
        unit = jnp.where(lane < sub + 8 * t, tile, jnp.where(lane == sub + 8 * t, 1.0, 0.0))
        out.append(unit * (1.0 / jnp.sqrt(diag)))
    return jnp.concatenate(out, axis=0)


def factor_kernel(gram, linv):
    linv[...] = inverse_factor(gram[...].reshape(NV, NV))


def finish_kernel(gram, y, out):
    linv = inverse_factor(gram[...].reshape(NV, NV))
    out[0] = times_inverse(y[0], linv)
    out[1] = times_inverse(y[1], linv)


def split(v):
    hi = v.astype(BF16)
    lo = (v - hi.astype(F32)).astype(BF16)
    return hi, lo


def product_kernel(places, blocks, row_side, col_side, rows, cols, wcol, xrow, flipped):
    step = pl.program_id(0)

    @pl.when(step == 0)
    def _():
        @pl.loop(0, 16)
        def _(i):
            hi, lo = split(col_side[i])
            wcol[i] = jnp.concatenate([jnp.concatenate([hi, lo], axis=1)] * 2, axis=0)
            flipped[i] = jnp.zeros((NV, BLK), F32)

        @pl.loop(0, 32)
        def _(i):
            hi, lo = split(row_side[i].T)
            xrow[i] = jnp.concatenate([hi, lo], axis=1)
            rows[i] = jnp.zeros((BLK, NV), F32)

    for b in range(CHUNK):
        k = step * CHUNK + b
        r = places[0, k]
        c = places[1, k]
        hi, lo = split(blocks[b])
        flat = jnp.concatenate([hi, lo], axis=1)
        d = jnp.dot(flat, wcol[c], preferred_element_type=F32)
        rows[r] += d[:, :NV] + d[:, NV:]
        e = jnp.dot(xrow[r], jnp.concatenate([flat, flat], axis=0), preferred_element_type=F32)
        flipped[c] += e[:, :BLK] + e[:, BLK:]

    @pl.when(step == pl.num_programs(0) - 1)
    def _():
        @pl.loop(0, 16)
        def _(i):
            cols[i] = flipped[i].T


def products(values, places, rowbuf, colbuf):
    listed = values.shape[0]
    whole = lambda n: pl.BlockSpec((n, BLK, NV), lambda i, p: (0, 0, 0), pipeline_mode=pl.Buffered(1))
    rows, cols = pl.pallas_call(
        product_kernel,
        out_shape=(
            jax.ShapeDtypeStruct((32, BLK, NV), F32),
            jax.ShapeDtypeStruct((16, BLK, NV), F32),
        ),
        grid_spec=pltpu.PrefetchScalarGridSpec(
            num_scalar_prefetch=1,
            grid=(listed // CHUNK,),
            in_specs=[
                pl.BlockSpec((CHUNK, BLK, BLK), lambda i, p: (i, 0, 0)),
                whole(32),
                whole(16),
            ],
            out_specs=(whole(32), whole(16)),
            scratch_shapes=[
                pltpu.VMEM((16, 2 * BLK, 2 * NV), BF16),
                pltpu.VMEM((32, NV, 2 * BLK), BF16),
                pltpu.VMEM((16, NV, BLK), F32),
            ],
        ),
        compiler_params=pltpu.CompilerParams(vmem_limit_bytes=40 << 20),
        name="tile_products",
    )(places, values, rowbuf.reshape(32, BLK, NV), colbuf.reshape(16, BLK, NV))
    return rows.reshape(NCOL, GROUP, NV), cols.reshape(NROW, GROUP, NV)


VM = pl.BlockSpec(memory_space=pltpu.VMEM)


def remote_call(kernel, name, cid, ins, outs, scratch):
    return pl.pallas_call(
        kernel,
        out_shape=tuple(jax.ShapeDtypeStruct(s, F32) for s in outs),
        in_specs=[VM] * ins,
        out_specs=tuple([VM] * len(outs)),
        scratch_shapes=scratch,
        compiler_params=pltpu.CompilerParams(
            collective_id=cid, has_side_effects=True, vmem_limit_bytes=40 << 20
        ),
        name=name,
    )


def local(blocks, coords, vectors):
    values = blocks.reshape(blocks.shape[2], BLK, BLK)
    places = coords.reshape(2, coords.shape[3])
    row_shape = (NCOL, GROUP, NV)
    col_shape = (NROW, GROUP, NV)
    gram_shape = (NCOL, 8, NV)
    rowbuf, colbuf = remote_call(gather_kernel, "gather", 0, 1, [row_shape, col_shape], GATHER_SEMS)(vectors)
    rows, cols = products(values, places, rowbuf, colbuf)
    rowbuf, colbuf, gram = remote_call(
        middle_kernel,
        "middle",
        1,
        2,
        [row_shape, col_shape, gram_shape],
        RS_SCRATCH + [pltpu.VMEM((2, GROUP, NV), F32)] + GATHER_SEMS + GRAM_SCRATCH,
    )(rows, cols)
    linv = pl.pallas_call(
        factor_kernel,
        out_shape=jax.ShapeDtypeStruct((NV, NV), F32),
        name="factor",
    )(gram)
    rows, cols = products(values, places, rowbuf, colbuf)
    y, gram = remote_call(
        last_kernel,
        "last",
        2,
        3,
        [(2, GROUP, NV), gram_shape],
        RS_SCRATCH + GRAM_SCRATCH,
    )(rows, cols, linv)
    return pl.pallas_call(
        finish_kernel,
        out_shape=jax.ShapeDtypeStruct((2, GROUP, NV), F32),
        name="finish",
    )(gram, y)


def solution(mesh):
    return jax.shard_map(
        local,
        mesh=mesh,
        in_specs=(
            P("row", "col", None, None, None),
            P("row", "col", None, None),
            P(None, ("row", "col"), None),
        ),
        out_specs=P(None, ("row", "col"), None),
        check_vma=False,
    )
```

```python
import functools

import jax
import jax.numpy as jnp
from jax import lax
from jax.experimental import pallas as pl
from jax.experimental.pallas import tpu as pltpu
from jax.sharding import PartitionSpec as P

MESH = pl.DeviceIdType.MESH
HIGH = lax.Precision.HIGHEST
F32 = jnp.float32
BF16 = jnp.bfloat16

GROUP = 256
NV = 128
BLK = 128
NROW = 8
NCOL = 16
CHUNK = 17
VM = pl.BlockSpec(memory_space=pltpu.VMEM)
LIFT = 2.0**20


class Where:
    def __init__(self):
        self.r = lax.axis_index("row")
        self.c = lax.axis_index("col")
        self.z = self.r // 2
        self.yl = self.r % 2
        self.yh = self.c // 8
        self.x = (self.c // 2) % 4
        self.core = self.c % 2

    def zr(self, dz, other=False):
        yl = 1 - self.yl if other else self.yl
        return ((self.z + dz) % 4) * 2 + yl

    def xc(self, dx, other_y=False, other_core=False):
        yh = 1 - self.yh if other_y else self.yh
        core = 1 - self.core if other_core else self.core
        return (yh * 4 + (self.x + dx) % 4) * 2 + core

    def neighbours(self):
        out = [(self.zr(dz), self.c) for dz in (1, 2, 3)]
        out.append((self.zr(0, True), self.c))
        out += [(self.r, self.xc(dx)) for dx in (1, 2, 3)]
        out.append((self.r, self.xc(0, True)))
        out.append((self.r, self.xc(0, False, True)))
        return out

    def all_group(self):
        out = [((self.r + d) % NROW, self.c) for d in range(1, NROW)]
        out += [(self.r, (self.c + d) % NCOL) for d in range(1, NCOL)]
        return out


def entry_barrier(partners):
    barrier = pltpu.get_barrier_semaphore()
    for p in partners:
        pl.semaphore_signal(barrier, inc=1, device_id=p, device_id_type=MESH)
    pl.semaphore_wait(barrier, len(partners))


def rcopy(src, dst, send, recv, dev):
    return pltpu.make_async_remote_copy(
        src_ref=src,
        dst_ref=dst,
        send_sem=send,
        recv_sem=recv,
        device_id=dev,
        device_id_type=MESH,
    )


class Gather:
    def __init__(self, w, up, lo, rowbuf, colbuf, su, ru, sl, rl):
        self.w, self.up, self.lo = w, up, lo
        self.rowbuf, self.colbuf = rowbuf, colbuf
        self.su, self.ru, self.sl, self.rl = su, ru, sl, rl
        self.sent = []
        self.nu = 0
        self.nl = 0

    def send_u(self, src, piece, dev):
        cp = rcopy(src, self.rowbuf.at[piece], self.su.at[self.nu], self.ru.at[piece], dev)
        self.nu += 1
        cp.start()
        self.sent.append(cp)

    def send_l(self, src, piece, dev):
        cp = rcopy(src, self.colbuf.at[piece], self.sl.at[self.nl], self.rl.at[piece], dev)
        self.nl += 1
        cp.start()
        self.sent.append(cp)

    def wait_u(self, piece):
        ref = self.rowbuf.at[piece]
        rcopy(ref, ref, self.su.at[0], self.ru.at[piece], (self.w.r, self.w.xc(0, True))).wait_recv()

    def wait_l(self, piece):
        ref = self.colbuf.at[piece]
        rcopy(ref, ref, self.sl.at[0], self.rl.at[piece], (self.w.zr(0, True), self.w.c)).wait_recv()

    def start(self):
        w = self.w
        self.send_u(self.up, w.c, (w.r, w.xc(0, True)))
        self.send_l(self.lo, w.r, (w.zr(0, True), w.c))
        for d in (2, 1, 3):
            self.send_u(self.up, w.c, (w.r, w.xc(d)))
            self.send_l(self.lo, w.r, (w.zr(d), w.c))
        self.send_u(self.up, w.c, (w.r, w.xc(0, False, True)))
        self.rowbuf[w.c] = self.up[...]
        self.colbuf[w.r] = self.lo[...]

    def forward_y(self):
        w = self.w
        pu = w.xc(0, True)
        ql = w.zr(0, True)
        self.wait_l(ql)
        for d in (2, 1, 3):
            self.send_l(self.colbuf.at[ql], ql, (w.zr(d), w.c))
        self.wait_u(pu)
        for d in (2, 1, 3):
            self.send_u(self.rowbuf.at[pu], pu, (w.r, w.xc(d)))
        self.send_u(self.rowbuf.at[pu], pu, (w.r, w.xc(0, False, True)))

    def forward_x(self, other_y):
        w = self.w
        for d in (1, 3, 2):
            p = w.xc(d, other_y)
            self.wait_u(p)
            self.send_u(self.rowbuf.at[p], p, (w.r, w.xc(0, False, True)))

    def finish(self):
        w = self.w
        for other in (False, True):
            for d in (1, 2, 3):
                self.wait_l(w.zr(d, other))
        for other in (False, True):
            for d in (0, 1, 2, 3):
                self.wait_u(w.xc(d, other, True))
        for cp in self.sent:
            cp.wait_send()


def gather_kernel(vec, rowbuf, colbuf, su, ru, sl, rl):
    w = Where()
    entry_barrier(w.neighbours())
    g = Gather(w, vec.at[0], vec.at[1], rowbuf, colbuf, su, ru, sl, rl)
    g.start()
    g.forward_y()
    g.forward_x(False)
    g.forward_x(True)
    g.finish()


GATHER_SEMS = [
    pltpu.SemaphoreType.DMA((15,)),
    pltpu.SemaphoreType.DMA((16,)),
    pltpu.SemaphoreType.DMA((7,)),
    pltpu.SemaphoreType.DMA((8,)),
]


def reduce_scatter(w, rows, cols, acc, sib, xbuf, yhbuf, zbuf, ylbuf, mid, s_s, r_s, s_x, r_x, s_z, r_z, s_y, r_y, between=None):
    sent = []
    sibling = (w.r, w.xc(0, False, True))
    order = [(d, o) for d in (2, 1, 3, 0) for o in (True, False)]
    for i, (d, o) in enumerate(order):
        cp = rcopy(rows.at[w.xc(d, o, True)], sib.at[i], s_s.at[i], r_s.at[i], sibling)
        cp.start()
        sent.append(cp)
    for i, d in enumerate((2, 1, 3)):
        for j, o in enumerate((True, False)):
            cp = rcopy(cols.at[w.zr(d, o)], zbuf.at[i, j], s_z.at[i, j], r_z.at[i, j], (w.zr(d), w.c))
            cp.start()
            sent.append(cp)
    for i, (d, o) in enumerate(order):
        sent[i].wait_recv()
        acc[i] = rows[w.xc(d, o)] + sib[i]
        if d:
            k, j = i // 2, i % 2
            cp = rcopy(acc.at[i], xbuf.at[k, j], s_x.at[k, j], r_x.at[k, j], (w.r, w.xc(d)))
            cp.start()
            sent.append(cp)
    zc = [c for c in sent[8:14]]
    xc = [c for c in sent[14:20]]
    if between is not None:
        between()
    for i in range(3):
        zc[2 * i].wait_recv()
    mid[0] = cols[w.zr(0, True)] + zbuf[0, 0] + zbuf[1, 0] + zbuf[2, 0]
    cl = rcopy(mid.at[0], ylbuf, s_y.at[0], r_y.at[0], (w.zr(0, True), w.c))
    cl.start()
    for i in range(3):
        xc[2 * i].wait_recv()
    mid[1] = acc[6] + xbuf[0, 0] + xbuf[1, 0] + xbuf[2, 0]
    cu = rcopy(mid.at[1], yhbuf, s_y.at[1], r_y.at[1], (w.r, w.xc(0, True)))
    cu.start()
    for i in range(3):
        zc[2 * i + 1].wait_recv()
    lower = cols[w.zr(0)] + zbuf[0, 1] + zbuf[1, 1] + zbuf[2, 1]
    mid[2] = lower
    for i in range(3):
        xc[2 * i + 1].wait_recv()
    mid[3] = acc[7] + xbuf[0, 1] + xbuf[1, 1] + xbuf[2, 1]
    cl.wait_recv()
    lower = mid[2] + ylbuf[...]
    cu.wait_recv()
    upper = mid[3] + yhbuf[...]
    for cp in sent:
        cp.wait_send()
    cl.wait_send()
    cu.wait_send()
    return upper, lower


RS_SCRATCH = [
    pltpu.VMEM((8, GROUP, NV), F32),
    pltpu.VMEM((8, GROUP, NV), F32),
    pltpu.VMEM((3, 2, GROUP, NV), F32),
    pltpu.VMEM((GROUP, NV), F32),
    pltpu.VMEM((3, 2, GROUP, NV), F32),
    pltpu.VMEM((GROUP, NV), F32),
    pltpu.VMEM((4, GROUP, NV), F32),
    pltpu.SemaphoreType.DMA((8,)),
    pltpu.SemaphoreType.DMA((8,)),
    pltpu.SemaphoreType.DMA((3, 2)),
    pltpu.SemaphoreType.DMA((3, 2)),
    pltpu.SemaphoreType.DMA((3, 2)),
    pltpu.SemaphoreType.DMA((3, 2)),
    pltpu.SemaphoreType.DMA((2,)),
    pltpu.SemaphoreType.DMA((2,)),
]


class GramSum:
    def __init__(self, w, part, g1, s1, g2, s2, full, ss, rr):
        self.w, self.part, self.g1, self.s1, self.g2, self.s2, self.full = w, part, g1, s1, g2, s2, full
        self.ss, self.rr = ss, rr
        self.sent = []

    def exchange(self, lo, count, src_of, dst, me, dev_of):
        cps = []
        for d in range(1, count):
            cp = rcopy(src_of(d), dst.at[me], self.ss.at[lo + d], self.rr.at[lo + d], dev_of(d))
            cp.start()
            cps.append(cp)
        self.sent += cps
        return cps

    def phase1(self):
        w = self.w

        def src(d):
            return self.part.at[(w.c + d) % NCOL]

        self.cps = self.exchange(0, NCOL, src, self.g1, w.c, lambda d: (w.r, (w.c + d) % NCOL))
        self.g1[w.c] = self.part[w.c]

    def phase2(self):
        w = self.w
        for cp in self.cps:
            cp.wait_recv()
        total = self.g1[0]
        for i in range(1, NCOL):
            total = total + self.g1[i]
        self.s1[...] = total
        self.cps = self.exchange(NCOL, NROW, lambda d: self.s1, self.g2, w.r, lambda d: ((w.r + d) % NROW, w.c))
        self.g2[w.r] = total

    def phase3(self):
        w = self.w
        for cp in self.cps:
            cp.wait_recv()
        total = self.g2[0]
        for i in range(1, NROW):
            total = total + self.g2[i]
        total = total * (1.0 / (2 * GROUP * NROW * NCOL))
        self.s2[...] = total
        self.cps = self.exchange(
            NCOL + NROW, NCOL, lambda d: self.s2, self.full, w.c, lambda d: (w.r, (w.c + d) % NCOL)
        )
        self.full[w.c] = total

    def finish(self):
        for cp in self.cps:
            cp.wait_recv()
        for cp in self.sent:
            cp.wait_send()


GRAM_SCRATCH = [
    pltpu.VMEM((NCOL, 8, NV), F32),
    pltpu.VMEM((NCOL, 8, NV), F32),
    pltpu.VMEM((8, NV), F32),
    pltpu.VMEM((NROW, 8, NV), F32),
    pltpu.VMEM((8, NV), F32),
    pltpu.SemaphoreType.DMA((2 * NCOL + NROW,)),
    pltpu.SemaphoreType.DMA((2 * NCOL + NROW,)),
]


def self_product(v):
    return lax.dot_general(v, v, (((0,), (0,)), ((), ())), precision=HIGH, preferred_element_type=F32)


def middle_kernel(rows, cols, rowbuf, colbuf, gram, acc, sib, xbuf, yhbuf, zbuf, ylbuf, mid, s_s, r_s, s_x, r_x, s_z, r_z, s_y, r_y, both, su, ru, sl, rl, part, g1, s1, g2, s2, ss, rr):
    w = Where()
    entry_barrier(w.all_group())
    upper, lower = reduce_scatter(w, rows, cols, acc, sib, xbuf, yhbuf, zbuf, ylbuf, mid, s_s, r_s, s_x, r_x, s_z, r_z, s_y, r_y)
    both[0] = upper * LIFT
    both[1] = lower * LIFT
    g = Gather(w, both.at[0], both.at[1], rowbuf, colbuf, su, ru, sl, rl)
    g.start()
    part[...] = (self_product(both[0]) + self_product(both[1])).reshape(NCOL, 8, NV)
    s = GramSum(w, part, g1, s1, g2, s2, gram, ss, rr)
    s.phase1()
    g.forward_y()
    s.phase2()
    g.forward_x(False)
    s.phase3()
    g.forward_x(True)
    g.finish()
    s.finish()


def times_inverse(v, linv):
    return lax.dot_general(v, linv, (((1,), (1,)), ((), ())), precision=HIGH, preferred_element_type=F32)


def last_kernel(rows, cols, gram_before, out, gram, acc, sib, xbuf, yhbuf, zbuf, ylbuf, mid, s_s, r_s, s_x, r_x, s_z, r_z, s_y, r_y, part, g1, s1, g2, s2, ss, rr, linv):
    w = Where()
    entry_barrier(w.all_group())

    def between():
        linv[...] = inverse_factor(gram_before[...].reshape(NV, NV))

    upper, lower = reduce_scatter(w, rows, cols, acc, sib, xbuf, yhbuf, zbuf, ylbuf, mid, s_s, r_s, s_x, r_x, s_z, r_z, s_y, r_y, between)
    out[0] = times_inverse(upper, linv[...])
    out[1] = times_inverse(lower, linv[...])
    part[...] = (self_product(out[0]) + self_product(out[1])).reshape(NCOL, 8, NV)
    s = GramSum(w, part, g1, s1, g2, s2, gram, ss, rr)
    s.phase1()
    s.phase2()
    s.phase3()
    s.finish()


def inverse_factor(gram):
    lane = lax.broadcasted_iota(jnp.int32, (8, NV), 1)
    sub = lax.broadcasted_iota(jnp.int32, (8, NV), 0)
    row = lax.broadcasted_iota(jnp.int32, (NV, NV), 0)
    inside = lax.broadcasted_iota(jnp.int32, (NV, NV), 1) < 8
    def block(it, w):
        top = w[:8]
        cols = [jnp.broadcast_to(w[:, i:i+1], (NV, NV)) for i in range(8)]
        b = [c[:8] for c in cols]
        x = jnp.where(lane < 8, jnp.where(lane == sub, 1.0, 0.0), top)
        fin = x
        for j in range(8):
            here = sub == j
            p = jnp.broadcast_to(b[j][j:j+1], (8, NV))
            inv = 1.0 / p
            xr = jnp.broadcast_to(x[j:j+1], (8, NV))
            fin = jnp.where(here, xr * (1.0 / jnp.sqrt(p)), fin)
            xs = xr * inv
            cj = b[j]
            x = jnp.where(here, xs, x - cj * xs)
            for k in range(j + 1, 8):
                bs = jnp.broadcast_to(b[k][j:j+1], (8, NV)) * inv
                b[k] = jnp.where(here, bs, b[k] - cj * bs)
        upd = jnp.where(inside, 0.0, w)
        for i in range(8):
            upd = upd - cols[i] * jnp.broadcast_to(x[i:i+1], (NV, NV))
        w = jnp.where(row < NV - 8 * it, upd, w)
        w = jnp.concatenate([w[8:], fin], axis=0)
        return pltpu.roll(w, NV - 8, 1)
    w = lax.fori_loop(0, 16, block, gram)
    return jnp.where(lax.broadcasted_iota(jnp.int32, (NV, NV), 1) <= row, w, 0.0)


def finish_kernel(gram, y, out):
    linv = inverse_factor(gram[...].reshape(NV, NV))
    out[0] = times_inverse(y[0], linv)
    out[1] = times_inverse(y[1], linv)


def split(v):
    hi = v.astype(BF16)
    lo = (v - hi.astype(F32)).astype(BF16)
    return hi, lo


def product_kernel(places, blocks, row_side, col_side, rows, cols, wcol, xrow, flipped, held, sem):
    listed = blocks.shape[0]
    steps = listed // CHUNK

    def piece(i):
        part = pl.ds(i * CHUNK, CHUNK)
        return pltpu.make_async_copy(blocks.at[part], held.at[part], sem.at[i])

    for i in range(steps):
        piece(i).start()

    def col_piece(i, carry):
        hi, lo = split(col_side[i])
        wcol[i] = jnp.concatenate([jnp.concatenate([hi, lo], axis=1)] * 2, axis=0)
        flipped[i] = jnp.zeros((NV, BLK), F32)
        return carry

    def row_piece(i, carry):
        hi, lo = split(row_side[i].T)
        xrow[i] = jnp.concatenate([hi, lo], axis=1)
        rows[i] = jnp.zeros((BLK, NV), F32)
        return carry

    lax.fori_loop(0, 16, col_piece, 0, unroll=8)
    lax.fori_loop(0, 32, row_piece, 0, unroll=8)

    def step(i, carry):
        piece(i).wait()
        for b in range(CHUNK):
            k = i * CHUNK + b
            r = places[0, k]
            c = places[1, k]
            hi, lo = split(held[k])
            flat = jnp.concatenate([hi, lo], axis=1)
            d = jnp.dot(flat, wcol[c], preferred_element_type=F32)
            rows[r] += d[:, :NV] + d[:, NV:]
            e = jnp.dot(xrow[r], jnp.concatenate([flat, flat], axis=0), preferred_element_type=F32)
            flipped[c] += e[:, :BLK] + e[:, BLK:]
        return carry

    lax.fori_loop(0, steps, step, 0)

    def back(i, carry):
        cols[i] = flipped[i].T
        return carry

    lax.fori_loop(0, 16, back, 0, unroll=8)


def products(values, places, rowbuf, colbuf):
    listed = values.shape[0]
    rows, cols = pl.pallas_call(
        product_kernel,
        out_shape=(
            jax.ShapeDtypeStruct((32, BLK, NV), F32),
            jax.ShapeDtypeStruct((16, BLK, NV), F32),
        ),
        in_specs=[
            pl.BlockSpec(memory_space=pltpu.SMEM),
            pl.BlockSpec(memory_space=pl.ANY),
            VM,
            VM,
        ],
        out_specs=(VM, VM),
        scratch_shapes=[
            pltpu.VMEM((16, 2 * BLK, 2 * NV), BF16),
            pltpu.VMEM((32, NV, 2 * BLK), BF16),
            pltpu.VMEM((16, NV, BLK), F32),
            pltpu.VMEM((listed, BLK, BLK), F32),
            pltpu.SemaphoreType.DMA((listed // CHUNK,)),
        ],
        compiler_params=pltpu.CompilerParams(vmem_limit_bytes=40 << 20),
        name="tile_products",
    )(places, values, rowbuf.reshape(32, BLK, NV), colbuf.reshape(16, BLK, NV))
    return rows.reshape(NCOL, GROUP, NV), cols.reshape(NROW, GROUP, NV)


def remote_call(kernel, name, cid, ins, outs, scratch):
    return pl.pallas_call(
        kernel,
        out_shape=tuple(jax.ShapeDtypeStruct(s, F32) for s in outs),
        in_specs=[VM] * ins,
        out_specs=tuple([VM] * len(outs)),
        scratch_shapes=scratch,
        compiler_params=pltpu.CompilerParams(
            collective_id=cid, has_side_effects=True, vmem_limit_bytes=40 << 20
        ),
        name=name,
    )


def local(blocks, coords, vectors):
    values = blocks.reshape(blocks.shape[2], BLK, BLK)
    places = coords.reshape(2, coords.shape[3])
    row_shape = (NCOL, GROUP, NV)
    col_shape = (NROW, GROUP, NV)
    gram_shape = (NCOL, 8, NV)
    rowbuf, colbuf = remote_call(gather_kernel, "gather", 0, 1, [row_shape, col_shape], GATHER_SEMS)(vectors)
    rows, cols = products(values, places, rowbuf, colbuf)
    rowbuf, colbuf, gram = remote_call(
        middle_kernel,
        "middle",
        1,
        2,
        [row_shape, col_shape, gram_shape],
        RS_SCRATCH + [pltpu.VMEM((2, GROUP, NV), F32)] + GATHER_SEMS + GRAM_SCRATCH,
    )(rows, cols)
    rows, cols = products(values, places, rowbuf, colbuf)
    y, gram = remote_call(
        last_kernel,
        "last",
        2,
        3,
        [(2, GROUP, NV), gram_shape],
        RS_SCRATCH + GRAM_SCRATCH + [pltpu.VMEM((NV, NV), F32)],
    )(rows, cols, gram)
    return pl.pallas_call(
        finish_kernel,
        out_shape=jax.ShapeDtypeStruct((2, GROUP, NV), F32),
        name="finish",
    )(gram, y)


def solution(mesh):
    return jax.shard_map(
        local,
        mesh=mesh,
        in_specs=(
            P("row", "col", None, None, None),
            P("row", "col", None, None),
            P(None, ("row", "col"), None),
        ),
        out_specs=P(None, ("row", "col"), None),
        check_vma=False,
    )
```

```python
import functools

import jax
import jax.numpy as jnp
from jax import lax
from jax.experimental import pallas as pl
from jax.experimental.pallas import tpu as pltpu
from jax.sharding import PartitionSpec as P

MESH = pl.DeviceIdType.MESH
HIGH = lax.Precision.HIGHEST
F32 = jnp.float32
BF16 = jnp.bfloat16

GROUP = 256
NV = 128
BLK = 128
NROW = 8
NCOL = 16
CHUNK = 17
VM = pl.BlockSpec(memory_space=pltpu.VMEM)
LIFT = 2.0**20


class Where:
    def __init__(self):
        self.r = lax.axis_index("row")
        self.c = lax.axis_index("col")
        self.z = self.r // 2
        self.yl = self.r % 2
        self.yh = self.c // 8
        self.x = (self.c // 2) % 4
        self.core = self.c % 2

    def zr(self, dz, other=False):
        yl = 1 - self.yl if other else self.yl
        return ((self.z + dz) % 4) * 2 + yl

    def xc(self, dx, other_y=False, other_core=False):
        yh = 1 - self.yh if other_y else self.yh
        core = 1 - self.core if other_core else self.core
        return (yh * 4 + (self.x + dx) % 4) * 2 + core

    def neighbours(self):
        out = [(self.zr(dz), self.c) for dz in (1, 3)]
        out.append((self.zr(0, True), self.c))
        out += [(self.r, self.xc(dx)) for dx in (1, 3)]
        out.append((self.r, self.xc(0, True)))
        out.append((self.r, self.xc(0, False, True)))
        return out

    def all_group(self):
        out = [((self.r + d) % NROW, self.c) for d in range(1, NROW)]
        out += [(self.r, (self.c + d) % NCOL) for d in range(1, NCOL)]
        return out


def entry_barrier(partners):
    barrier = pltpu.get_barrier_semaphore()
    for p in partners:
        pl.semaphore_signal(barrier, inc=1, device_id=p, device_id_type=MESH)
    pl.semaphore_wait(barrier, len(partners))


def rcopy(src, dst, send, recv, dev):
    return pltpu.make_async_remote_copy(
        src_ref=src,
        dst_ref=dst,
        send_sem=send,
        recv_sem=recv,
        device_id=dev,
        device_id_type=MESH,
    )


HALF = GROUP // 2


def half(ref, h):
    return ref.at[pl.ds(h * HALF, HALF)]


class Posts:
    def __init__(self, pool):
        self.pool = pool
        self.sent = []

    def post(self, src, dst, recv, dev):
        cp = rcopy(src, dst, self.pool.at[len(self.sent)], recv, dev)
        cp.start()
        self.sent.append(cp)
        return cp

    def arrived(self, ref, recv, dev):
        rcopy(ref, ref, self.pool.at[0], recv, dev).wait_recv()

    def drain(self):
        for cp in self.sent:
            cp.wait_send()
        self.sent = []


class Gather:
    def __init__(self, w, posts, up, lo, rowbuf, colbuf, ru, rl):
        self.w, self.posts, self.up, self.lo = w, posts, up, lo
        self.rowbuf, self.colbuf, self.ru, self.rl = rowbuf, colbuf, ru, rl
        self.sibling = (w.r, w.xc(0, False, True))

    def send_u(self, src, p, dev):
        self.posts.post(src, self.rowbuf.at[p], self.ru.at[p], dev)

    def send_l(self, src, q, dev):
        self.posts.post(src, self.colbuf.at[q], self.rl.at[q], dev)

    def wait_u(self, p):
        self.posts.arrived(self.rowbuf.at[p], self.ru.at[p], self.sibling)

    def wait_l(self, q):
        self.posts.arrived(self.colbuf.at[q], self.rl.at[q], self.sibling)

    def start_l(self):
        w = self.w
        self.send_l(self.lo, w.r, (w.zr(0, True), w.c))
        for d in (2, 1, 3):
            self.send_l(self.lo, w.r, (w.zr(d), w.c))
        self.colbuf[w.r] = self.lo[...]

    def start_u(self):
        w = self.w
        self.send_u(self.up, w.c, (w.r, w.xc(0, True)))
        for d in (2, 1, 3):
            self.send_u(self.up, w.c, (w.r, w.xc(d)))
        self.send_u(self.up, w.c, self.sibling)
        self.rowbuf[w.c] = self.up[...]

    def from_y_l(self):
        w = self.w
        q = w.zr(0, True)
        self.wait_l(q)
        for d in (2, 1, 3):
            self.send_l(self.colbuf.at[q], q, (w.zr(d), w.c))

    def from_y_u(self):
        w = self.w
        p = w.xc(0, True)
        self.wait_u(p)
        for d in (2, 1, 3):
            self.send_u(self.rowbuf.at[p], p, (w.r, w.xc(d)))
        self.send_u(self.rowbuf.at[p], p, self.sibling)

    def from_x(self, other):
        for d in (1, 3, 2):
            p = self.w.xc(d, other)
            self.wait_u(p)
            self.send_u(self.rowbuf.at[p], p, self.sibling)

    def rest_l(self):
        for other in (False, True):
            for d in (1, 2, 3):
                self.wait_l(self.w.zr(d, other))

    def rest_u(self):
        for other in (False, True):
            for d in range(4):
                self.wait_u(self.w.xc(d, other, True))


GATHER_SEMS = [pltpu.SemaphoreType.DMA((NCOL,)), pltpu.SemaphoreType.DMA((NROW,))]


class Ring:
    def __init__(self, posts, dev, part, dep, rel, fin, r_rel, r_fin):
        self.posts, self.dev, self.part = posts, dev, part
        self.dep, self.rel, self.fin = dep, rel, fin
        self.r_rel, self.r_fin = r_rel, r_fin

    def far(self, o):
        for k, s in enumerate((1, -1)):
            self.posts.post(half(self.part(2, o), k), self.rel.at[k, o], self.r_rel.at[k, o], self.dev(s))

    def near(self, o):
        for k, s in enumerate((1, -1)):
            h = 1 - k
            self.posts.post(half(self.part(s, o), h), half(self.fin.at[k, o], h), self.r_fin.at[k, o, h], self.dev(s))

    def through(self, o):
        for k, s in enumerate((1, -1)):
            self.posts.arrived(self.rel.at[k, o], self.r_rel.at[k, o], self.dev(s))
            self.dep[k, o] = half(self.part(s, o), k)[...] + self.rel[k, o]
            self.posts.post(self.dep.at[k, o], half(self.fin.at[k, o], k), self.r_fin.at[k, o, k], self.dev(s))

    def total(self, o):
        for k in (0, 1):
            for h in (0, 1):
                self.posts.arrived(half(self.fin.at[k, o], h), self.r_fin.at[k, o, h], self.dev(1))
        return self.part(0, o)[...] + self.fin[0, o] + self.fin[1, o]


def reduce_scatter(w, posts, rows, cols, scratch, flip, on_lower, on_upper, beside):
    acc, sib, r_sib, depx, relx, finx, r_relx, r_finx, depz, relz, finz, r_relz, r_finz, mid, ybuf, r_y = scratch
    sibling = (w.r, w.xc(0, False, True))
    slots = [(2, 1), (1, 1), (3, 1), (2, 0), (1, 0), (3, 0), (0, 1), (0, 0)]
    at = {s: i for i, s in enumerate(slots)}

    def xpart(d, o):
        return acc.at[at[d % 4, o]]

    def zpart(d, o):
        return cols.at[w.zr(d % 4, o == 1)]

    xr = Ring(posts, lambda s: (w.r, w.xc(s % 4)), xpart, depx, relx, finx, r_relx, r_finx)
    zr = Ring(posts, lambda s: (w.zr(s % 4), w.c), zpart, depz, relz, finz, r_relz, r_finz)

    def join(*ids):
        for i in ids:
            posts.arrived(sib.at[i], r_sib.at[i], sibling)
            d, o = slots[i]
            acc[i] = rows[w.xc(d, o == 1)] + sib[i]

    for i, (d, o) in enumerate(slots):
        posts.post(rows.at[w.xc(d, o == 1, True)], sib.at[i], r_sib.at[i], sibling)
    flip(0)
    join(0)
    xr.far(1)
    join(1, 2)
    xr.near(1)
    join(3)
    xr.far(0)
    join(4, 5)
    flip(1)
    zr.far(1)
    zr.near(1)
    zr.far(0)
    xr.through(1)
    xr.near(0)
    zr.near(0)
    join(6, 7)
    xr.through(0)
    beside(0)
    zr.through(1)
    zr.through(0)
    beside(1)
    mid[1] = xr.total(1)
    for h in (0, 1):
        posts.post(half(mid.at[1], h), half(ybuf.at[1], h), r_y.at[1, h], (w.r, w.xc(0, True)))
    beside(2)
    mid[0] = zr.total(1)
    for h in (0, 1):
        posts.post(half(mid.at[0], h), half(ybuf.at[0], h), r_y.at[0, h], (w.zr(0, True), w.c))
    mid[3] = xr.total(0)
    beside(3)
    for h in (0, 1):
        posts.arrived(half(ybuf.at[1], h), r_y.at[1, h], sibling)
    on_upper(mid[3] + ybuf[1])
    mid[2] = zr.total(0)
    for h in (0, 1):
        posts.arrived(half(ybuf.at[0], h), r_y.at[0, h], sibling)
    on_lower(mid[2] + ybuf[0])


RING_SCRATCH = [
    pltpu.VMEM((2, 2, HALF, NV), F32),
    pltpu.VMEM((2, 2, HALF, NV), F32),
    pltpu.VMEM((2, 2, GROUP, NV), F32),
    pltpu.SemaphoreType.DMA((2, 2)),
    pltpu.SemaphoreType.DMA((2, 2, 2)),
]
RS_SCRATCH = (
    [
        pltpu.VMEM((8, GROUP, NV), F32),
        pltpu.VMEM((8, GROUP, NV), F32),
        pltpu.SemaphoreType.DMA((8,)),
    ]
    + RING_SCRATCH
    + RING_SCRATCH
    + [
        pltpu.VMEM((4, GROUP, NV), F32),
        pltpu.VMEM((2, GROUP, NV), F32),
        pltpu.SemaphoreType.DMA((2, 2)),
    ]
)
POOL = pltpu.SemaphoreType.DMA((128,))


class GramSum:
    def __init__(self, w, posts, full, part, g1, s1, g2, s2, rr):
        self.w, self.posts, self.full = w, posts, full
        self.part, self.g1, self.s1, self.g2, self.s2, self.rr = part, g1, s1, g2, s2, rr

    def over_col(self, lo, src, dst):
        w = self.w
        self.cps = []
        for d in range(1, NCOL):
            to = (w.c + d) % NCOL
            self.cps.append(self.posts.post(src(to), dst.at[w.c], self.rr.at[lo + d], (w.r, to)))

    def join(self):
        for cp in self.cps:
            cp.wait_recv()

    def phase1(self):
        w = self.w
        self.over_col(0, lambda to: self.part.at[to], self.g1)
        self.g1[w.c] = self.part[w.c]

    def phase2(self):
        w = self.w
        self.join()
        total = self.g1[0]
        for i in range(1, NCOL):
            total = total + self.g1[i]
        self.s1[...] = total
        self.cps = []
        for d in range(1, NROW):
            to = ((w.r + d) % NROW, w.c)
            self.cps.append(self.posts.post(self.s1, self.g2.at[w.r], self.rr.at[NCOL + d], to))
        self.g2[w.r] = total

    def phase3(self):
        w = self.w
        self.join()
        total = self.g2[0]
        for i in range(1, NROW):
            total = total + self.g2[i]
        total = total * (1.0 / (2 * GROUP * NROW * NCOL))
        self.s2[...] = total
        self.over_col(NCOL + NROW, lambda to: self.s2, self.full)
        self.full[w.c] = total


GRAM_SCRATCH = [
    pltpu.VMEM((NCOL, 8, NV), F32),
    pltpu.VMEM((NCOL, 8, NV), F32),
    pltpu.VMEM((8, NV), F32),
    pltpu.VMEM((NROW, 8, NV), F32),
    pltpu.VMEM((8, NV), F32),
    pltpu.SemaphoreType.DMA((2 * NCOL + NROW,)),
]
NG = len(GRAM_SCRATCH)
NR = len(RS_SCRATCH)


def self_product(v):
    return lax.dot_general(v, v, (((0,), (0,)), ((), ())), precision=HIGH, preferred_element_type=F32)


def times_inverse(v, linv):
    return lax.dot_general(v, linv, (((1,), (1,)), ((), ())), precision=HIGH, preferred_element_type=F32)


def eliminate(gram, first, last):
    lane = lax.broadcasted_iota(jnp.int32, (8, NV), 1)
    sub = lax.broadcasted_iota(jnp.int32, (8, NV), 0)
    row = lax.broadcasted_iota(jnp.int32, (NV, NV), 0)
    inside = lax.broadcasted_iota(jnp.int32, (NV, NV), 1) < 8
    def block(it, w):
        top = w[:8]
        cols = [jnp.broadcast_to(w[:, i:i+1], (NV, NV)) for i in range(8)]
        b = [c[:8] for c in cols]
        x = jnp.where(lane < 8, jnp.where(lane == sub, 1.0, 0.0), top)
        fin = x
        for j in range(8):
            here = sub == j
            p = jnp.broadcast_to(b[j][j:j+1], (8, NV))
            inv = 1.0 / p
            xr = jnp.broadcast_to(x[j:j+1], (8, NV))
            fin = jnp.where(here, xr * (1.0 / jnp.sqrt(p)), fin)
            xs = xr * inv
            cj = b[j]
            x = jnp.where(here, xs, x - cj * xs)
            for k in range(j + 1, 8):
                bs = jnp.broadcast_to(b[k][j:j+1], (8, NV)) * inv
                b[k] = jnp.where(here, bs, b[k] - cj * bs)
        upd = jnp.where(inside, 0.0, w)
        for i in range(8):
            upd = upd - cols[i] * jnp.broadcast_to(x[i:i+1], (NV, NV))
        w = jnp.where(row < NV - 8 * it, upd, w)
        w = jnp.concatenate([w[8:], fin], axis=0)
        return pltpu.roll(w, NV - 8, 1)
    return lax.fori_loop(first, last, block, gram)


def lower_part(w):
    row = lax.broadcasted_iota(jnp.int32, (NV, NV), 0)
    return jnp.where(lax.broadcasted_iota(jnp.int32, (NV, NV), 1) <= row, w, 0.0)


def split(v):
    hi = v.astype(BF16)
    lo = (v - hi.astype(F32)).astype(BF16)
    return hi, lo


def link_kernel(places, links, ends, last_row, last_col):
    listed = places.shape[1]
    for i in range(32):
        last_row[i] = 0
    for i in range(16):
        last_col[i] = 0
    for k in range(listed):
        r = places[0, k]
        c = places[1, k]
        links[0, k] = last_row[r]
        links[1, k] = last_col[c]
        last_row[r] = k + 1
        last_col[c] = k + 1
    for i in range(32):
        ends[0, i] = last_row[i]
    for i in range(16):
        ends[1, i] = last_col[i]


class Tile:
    def __init__(self, places, links, ends, blocks, sem, flat, chain, wcol, xrow):
        self.places, self.links, self.ends, self.blocks, self.sem = places, links, ends, blocks, sem
        self.flat, self.chain, self.wcol, self.xrow = flat, chain, wcol, xrow
        self.steps = blocks.shape[0] // CHUNK

    def piece(self, i):
        return pltpu.make_async_copy(
            self.blocks.at[pl.ds(i * CHUNK, CHUNK)],
            self.chain.at[pl.ds(i * CHUNK + 1, CHUNK)],
            self.sem.at[i],
        )

    def fetch(self):
        for i in range(self.steps):
            self.piece(i).start()

    def convert(self, lo, hi):
        for i in range(lo, hi):
            self.piece(i).wait()

            def one(k, carry):
                hi_part, lo_part = split(self.chain[i * CHUNK + 1 + k])
                self.flat[i * CHUNK + k] = jnp.concatenate([hi_part, lo_part], axis=1)
                return carry

            lax.fori_loop(0, CHUNK, one, 0, unroll=CHUNK)

    def clear(self):
        self.chain[0] = jnp.zeros((BLK, BLK), F32)

    def take_cols(self, colbuf):
        def one(i, carry):
            hi, lo = split(colbuf[i])
            for h in (0, 1):
                a, b = hi[h * BLK : (h + 1) * BLK], lo[h * BLK : (h + 1) * BLK]
                self.wcol[2 * i + h] = jnp.concatenate([jnp.concatenate([a, b], axis=1)] * 2, axis=0)
            return carry

        lax.fori_loop(0, NROW, one, 0, unroll=4)

    def take_rows(self, rowbuf):
        def one(i, carry):
            hi, lo = split(rowbuf[i].T)
            for h in (0, 1):
                a, b = hi[:, h * BLK : (h + 1) * BLK], lo[:, h * BLK : (h + 1) * BLK]
                self.xrow[2 * i + h] = jnp.concatenate([a, b], axis=1)
            return carry

        lax.fori_loop(0, NCOL, one, 0, unroll=4)

    def direct(self, rows):
        def step(i, carry):
            for b in range(CHUNK):
                k = i * CHUNK + b
                d = jnp.dot(self.flat[k], self.wcol[self.places[1, k]], preferred_element_type=F32)
                self.chain[k + 1] = d[:, :NV] + d[:, NV:] + self.chain[self.links[0, k]]
            return carry

        lax.fori_loop(0, self.steps, step, 0)

        def out(i, carry):
            for h in (0, 1):
                rows[i, pl.ds(h * BLK, BLK)] = self.chain[self.ends[0, 2 * i + h]]
            return carry

        lax.fori_loop(0, NCOL, out, 0, unroll=4)

    def flip(self, lo, hi):
        def step(i, carry):
            for b in range(CHUNK):
                k = i * CHUNK + b
                flat = self.flat[k]
                e = jnp.dot(
                    self.xrow[self.places[0, k]],
                    jnp.concatenate([flat, flat], axis=0),
                    preferred_element_type=F32,
                )
                self.chain[k + 1] = e[:, :BLK] + e[:, BLK:] + self.chain[self.links[1, k]]
            return carry

        lax.fori_loop(lo, hi, step, 0)

    def flipped(self, cols):
        def out(i, carry):
            for h in (0, 1):
                cols[i, pl.ds(h * BLK, BLK)] = self.chain[self.ends[1, 2 * i + h]].T
            return carry

        lax.fori_loop(0, NROW, out, 0, unroll=4)


APP_SCRATCH = (
    [pltpu.VMEM((NCOL, GROUP, NV), F32), pltpu.VMEM((NROW, GROUP, NV), F32)]
    + GATHER_SEMS
    + RS_SCRATCH
    + [pltpu.VMEM((NCOL, 8, NV), F32)]
    + GRAM_SCRATCH
)
NA = len(APP_SCRATCH)


def whole_kernel(places, links, ends, blocks, vec, out, sem, flat, chain, wcol, xrow, rows, cols, pool, work, *scratch):
    w = Where()
    tile = Tile(places, links, ends, blocks, sem, flat, chain, wcol, xrow)
    tile.fetch()
    entry_barrier(w.all_group())
    posts = Posts(pool)

    class App:
        def __init__(self, refs, up, lo):
            self.rowbuf, self.colbuf, ru, rl = refs[:4]
            self.rs = refs[4 : 4 + NR]
            self.full = refs[4 + NR]
            self.gram = GramSum(w, posts, self.full, *refs[5 + NR :])
            self.part = refs[5 + NR]
            self.g = Gather(w, posts, up, lo, self.rowbuf, self.colbuf, ru, rl)

        def apply(self, on_lower, on_upper, beside):
            self.g.rest_l()
            tile.take_cols(self.colbuf)
            tile.direct(rows)

            def flip(i):
                if i == 0:
                    self.g.rest_u()
                    tile.take_rows(self.rowbuf)
                    tile.flip(0, tile.steps // 2)
                else:
                    tile.flip(tile.steps // 2, tile.steps)
                    tile.flipped(cols)

            reduce_scatter(w, posts, rows, cols, self.rs, flip, on_lower, on_upper, beside)

        def product(self, y):
            self.part[...] = (self_product(y[0]) + self_product(y[1])).reshape(NCOL, 8, NV)

    one = App(scratch[:NA], vec.at[0], vec.at[1])
    two = App(scratch[NA : 2 * NA], out.at[0], out.at[1])
    third = tile.steps // 3
    one.g.start_l()
    one.g.start_u()
    tile.clear()
    tile.convert(0, third)
    one.g.from_y_l()
    one.g.from_y_u()
    tile.convert(third, 2 * third)
    one.g.from_x(False)
    tile.convert(2 * third, tile.steps)
    one.g.from_x(True)

    def lower_one(v):
        out[1] = v * LIFT
        two.g.start_l()

    def upper_one(v):
        out[0] = v * LIFT
        two.g.start_u()

    one.apply(lower_one, upper_one, lambda i: None)
    one.product(out)
    one.gram.phase1()
    two.g.from_y_u()
    two.g.from_y_l()
    one.gram.phase2()
    two.g.from_x(False)
    one.gram.phase3()
    two.g.from_x(True)
    one.gram.join()
    posts.drain()

    def beside(i):
        state = one.full[...].reshape(NV, NV) if i == 0 else work[...]
        work[...] = eliminate(state, 4 * i, 4 * i + 4)

    def lower_two(v):
        out[1] = times_inverse(v, lower_part(work[...]))

    def upper_two(v):
        out[0] = times_inverse(v, lower_part(work[...]))

    two.apply(lower_two, upper_two, beside)
    two.product(out)
    two.gram.phase1()
    two.gram.phase2()
    two.gram.phase3()
    two.gram.join()
    linv = lower_part(eliminate(two.full[...].reshape(NV, NV), 0, 16))
    posts.drain()
    out[0] = times_inverse(out[0], linv)
    out[1] = times_inverse(out[1], linv)


def local(blocks, coords, vectors):
    values = blocks.reshape(blocks.shape[2], BLK, BLK)
    places = coords.reshape(2, coords.shape[3])
    listed = values.shape[0]
    scalars = pl.BlockSpec(memory_space=pltpu.SMEM)
    links, ends = pl.pallas_call(
        link_kernel,
        out_shape=(
            jax.ShapeDtypeStruct((2, listed), jnp.int32),
            jax.ShapeDtypeStruct((2, 32), jnp.int32),
        ),
        in_specs=[scalars],
        out_specs=(scalars, scalars),
        scratch_shapes=[pltpu.SMEM((32,), jnp.int32), pltpu.SMEM((16,), jnp.int32)],
        name="links",
    )(places)
    return pl.pallas_call(
        whole_kernel,
        out_shape=jax.ShapeDtypeStruct((2, GROUP, NV), F32),
        in_specs=[scalars] * 3 + [pl.BlockSpec(memory_space=pl.ANY), VM],
        out_specs=VM,
        scratch_shapes=[
            pltpu.SemaphoreType.DMA((listed // CHUNK,)),
            pltpu.VMEM((listed, BLK, 2 * BLK), BF16),
            pltpu.VMEM((listed + 1, BLK, BLK), F32),
            pltpu.VMEM((16, 2 * BLK, 2 * NV), BF16),
            pltpu.VMEM((32, NV, 2 * BLK), BF16),
            pltpu.VMEM((NCOL, GROUP, NV), F32),
            pltpu.VMEM((NROW, GROUP, NV), F32),
            POOL,
            pltpu.VMEM((NV, NV), F32),
        ]
        + APP_SCRATCH
        + APP_SCRATCH,
        compiler_params=pltpu.CompilerParams(
            collective_id=0, has_side_effects=True, vmem_limit_bytes=56 << 20
        ),
        name="whole",
    )(places, links, ends, values, vectors)


def solution(mesh):
    return jax.shard_map(
        local,
        mesh=mesh,
        in_specs=(
            P("row", "col", None, None, None),
            P("row", "col", None, None),
            P(None, ("row", "col"), None),
        ),
        out_specs=P(None, ("row", "col"), None),
        check_vma=False,
    )
```

```python
import functools

import jax
import jax.numpy as jnp
from jax import lax
from jax.experimental import pallas as pl
from jax.experimental.pallas import tpu as pltpu
from jax.sharding import PartitionSpec as P

MESH = pl.DeviceIdType.MESH
HIGH = lax.Precision.HIGHEST
F32 = jnp.float32
BF16 = jnp.bfloat16

GROUP = 256
NV = 128
BLK = 128
NROW = 8
NCOL = 16
CHUNK = 17
VM = pl.BlockSpec(memory_space=pltpu.VMEM)
LIFT = 2.0**20


class Where:
    def __init__(self):
        self.r = lax.axis_index("row")
        self.c = lax.axis_index("col")
        self.z = self.r // 2
        self.yl = self.r % 2
        self.yh = self.c // 8
        self.x = (self.c // 2) % 4
        self.core = self.c % 2

    def zr(self, dz, other=False):
        yl = 1 - self.yl if other else self.yl
        return ((self.z + dz) % 4) * 2 + yl

    def xc(self, dx, other_y=False, other_core=False):
        yh = 1 - self.yh if other_y else self.yh
        core = 1 - self.core if other_core else self.core
        return (yh * 4 + (self.x + dx) % 4) * 2 + core

    def neighbours(self):
        out = [(self.zr(dz), self.c) for dz in (1, 2, 3)]
        out.append((self.zr(0, True), self.c))
        out += [(self.r, self.xc(dx)) for dx in (1, 2, 3)]
        out.append((self.r, self.xc(0, True)))
        out.append((self.r, self.xc(0, False, True)))
        return out


def entry_barrier(partners):
    barrier = pltpu.get_barrier_semaphore()
    for p in partners:
        pl.semaphore_signal(barrier, inc=1, device_id=p, device_id_type=MESH)
    pl.semaphore_wait(barrier, len(partners))


def rcopy(src, dst, send, recv, dev):
    return pltpu.make_async_remote_copy(
        src_ref=src,
        dst_ref=dst,
        send_sem=send,
        recv_sem=recv,
        device_id=dev,
        device_id_type=MESH,
    )


HALF = GROUP // 2


def half(ref, h):
    return ref.at[pl.ds(h * HALF, HALF)]


class Posts:
    def __init__(self, pool):
        self.pool = pool
        self.sent = []
        self.oldest = 0

    def post(self, src, dst, recv, dev):
        slots = self.pool.shape[0]
        if len(self.sent) - self.oldest == slots:
            self.sent[self.oldest].wait_send()
            self.oldest += 1
        cp = rcopy(src, dst, self.pool.at[len(self.sent) % slots], recv, dev)
        cp.start()
        self.sent.append(cp)
        return cp

    def arrived(self, ref, recv, dev):
        rcopy(ref, ref, self.pool.at[0], recv, dev).wait_recv()

    def drain(self):
        for cp in self.sent[self.oldest :]:
            cp.wait_send()
        self.oldest = len(self.sent)


class Gather:
    def __init__(self, w, posts, up, lo, rowbuf, colbuf, r_u, r_sib, r_y, r_l):
        self.w, self.posts, self.up, self.lo = w, posts, up, lo
        self.rowbuf, self.colbuf = rowbuf, colbuf
        self.r_u, self.r_sib, self.r_y, self.r_l = r_u, r_sib.at[0], r_y.at[0], r_l.at[0]
        self.sibling = (w.r, w.xc(0, False, True))

    def send_u(self, src, p, dev):
        self.posts.post(src, self.rowbuf.at[p], self.r_u.at[p // 2], dev)

    def to_sibling(self, src, p):
        self.posts.post(src, self.rowbuf.at[p], self.r_sib, self.sibling)

    def send_l(self, src, q, recv, dev):
        self.posts.post(src, self.colbuf.at[q], recv, dev)

    def wait_u(self, p):
        self.posts.arrived(self.rowbuf.at[p], self.r_u.at[p // 2], self.sibling)

    def start_y_l(self):
        self.send_l(self.lo, self.w.r, self.r_y, (self.w.zr(0, True), self.w.c))

    def start_y_u(self):
        self.send_u(self.up, self.w.c, (self.w.r, self.w.xc(0, True)))

    def start_l(self):
        w = self.w
        for d in (2, 1, 3):
            self.send_l(self.lo, w.r, self.r_l, (w.zr(d), w.c))
        self.colbuf[w.r] = self.lo[...]

    def start_u(self):
        w = self.w
        for d in (2, 1, 3):
            self.send_u(self.up, w.c, (w.r, w.xc(d)))
        self.to_sibling(self.up, w.c)
        self.rowbuf[w.c] = self.up[...]

    def from_y_l(self):
        w = self.w
        q = w.zr(0, True)
        self.posts.arrived(self.colbuf.at[q], self.r_y, self.sibling)
        for d in (2, 1, 3):
            self.send_l(self.colbuf.at[q], q, self.r_l, (w.zr(d), w.c))

    def from_y_u(self):
        w = self.w
        p = w.xc(0, True)
        self.wait_u(p)
        for d in (2, 1, 3):
            self.send_u(self.rowbuf.at[p], p, (w.r, w.xc(d)))
        self.to_sibling(self.rowbuf.at[p], p)

    def from_x(self, other, steps=(1, 3, 2)):
        for d in steps:
            p = self.w.xc(d, other)
            self.wait_u(p)
            self.to_sibling(self.rowbuf.at[p], p)

    def rest_l(self):
        self.posts.arrived(self.colbuf.at[pl.ds(0, 6)], self.r_l, self.sibling)

    def rest_u(self):
        self.posts.arrived(self.rowbuf.at[pl.ds(0, 8)], self.r_sib, self.sibling)


GATHER_SEMS = [pltpu.SemaphoreType.DMA((n,)) for n in (8, 1, 1, 1)]
NS = len(GATHER_SEMS)


class Ring:
    def __init__(self, posts, dev, part, dep, rel, fin, r_rel, r_fin):
        self.posts, self.dev, self.part = posts, dev, part
        self.dep, self.rel, self.fin = dep, rel, fin
        self.r_rel, self.r_fin = r_rel, r_fin

    def far(self, o):
        for k, s in enumerate((1, -1)):
            self.posts.post(half(self.part(2, o), k), self.rel.at[o, k], self.r_rel.at[o], self.dev(s))

    def near(self, o):
        for k, s in enumerate((1, -1)):
            h = 1 - k
            self.posts.post(half(self.part(s, o), h), half(self.fin.at[o, k], h), self.r_fin.at[o], self.dev(s))

    def through(self, o):
        self.posts.arrived(self.rel.at[o], self.r_rel.at[o], self.dev(1))
        for k, s in enumerate((1, -1)):
            self.dep[o, k] = half(self.part(s, o), k)[...] + self.rel[o, k]
            self.posts.post(self.dep.at[o, k], half(self.fin.at[o, k], k), self.r_fin.at[o], self.dev(s))

    def total(self, o):
        self.posts.arrived(self.fin.at[o], self.r_fin.at[o], self.dev(1))
        return self.part(0, o)[...] + self.fin[o, 0] + self.fin[o, 1]


class Scatter:
    SLOTS = [(2, 1), (1, 1), (3, 1), (2, 0), (1, 0), (3, 0), (0, 1), (0, 0)]

    def __init__(self, w, posts, rows, cols, scratch):
        self.acc, self.sib, self.r_sib = scratch[:3]
        x, z = scratch[3:8], scratch[8:13]
        self.mid, self.ybuf, self.r_y = scratch[13:]
        self.w, self.posts, self.rows = w, posts, rows
        self.sibling = (w.r, w.xc(0, False, True))
        at = {slot: i for i, slot in enumerate(self.SLOTS)}
        self.x = Ring(posts, lambda s: (w.r, w.xc(s % 4)), lambda d, o: self.acc.at[at[d % 4, o]], *x)
        self.z = Ring(posts, lambda s: (w.zr(s % 4), w.c), lambda d, o: cols.at[w.zr(d % 4, o == 1)], *z)

    def siblings(self):
        for i, (d, o) in enumerate(self.SLOTS):
            src = self.rows.at[self.w.xc(d, o == 1, True)]
            self.posts.post(src, self.sib.at[i], self.r_sib.at[i], self.sibling)

    def join(self, *ids):
        for i in ids:
            self.posts.arrived(self.sib.at[i], self.r_sib.at[i], self.sibling)
            d, o = self.SLOTS[i]
            self.acc[i] = self.rows[self.w.xc(d, o == 1)] + self.sib[i]

    def far_x(self):
        self.join(0)
        self.x.far(1)
        self.join(1, 2)
        self.x.near(1)
        self.join(3)
        self.x.far(0)

    def far_z(self):
        self.z.far(1)
        self.z.near(1)
        self.z.far(0)

    def to_y(self, j, dev, value):
        self.mid[j] = value
        self.posts.post(self.mid.at[j], self.ybuf.at[j], self.r_y.at[j], dev)

    def to_y_x(self):
        self.to_y(1, (self.w.r, self.w.xc(0, True)), self.x.total(1))

    def to_y_z(self):
        self.to_y(0, (self.w.zr(0, True), self.w.c), self.z.total(1))

    def own(self, j, ring):
        self.mid[2 + j] = ring.total(0)

    def final(self, j):
        self.posts.arrived(self.ybuf.at[j], self.r_y.at[j], self.sibling)
        return self.mid[2 + j] + self.ybuf[j]


RING_SCRATCH = [
    pltpu.VMEM((2, 2, HALF, NV), F32),
    pltpu.VMEM((2, 2, HALF, NV), F32),
    pltpu.VMEM((2, 2, GROUP, NV), F32),
    pltpu.SemaphoreType.DMA((2,)),
    pltpu.SemaphoreType.DMA((2,)),
]
RS_SCRATCH = (
    [
        pltpu.VMEM((8, GROUP, NV), F32),
        pltpu.VMEM((8, GROUP, NV), F32),
        pltpu.SemaphoreType.DMA((8,)),
    ]
    + RING_SCRATCH
    + RING_SCRATCH
    + [
        pltpu.VMEM((4, GROUP, NV), F32),
        pltpu.VMEM((2, GROUP, NV), F32),
        pltpu.SemaphoreType.DMA((2,)),
    ]
)
POOLS = [pltpu.SemaphoreType.DMA((n,)) for n in (34, 22, 34)]


class GramSum:
    def __init__(self, w, full, part, g1, s1, g2, s2, send, recv):
        self.w, self.full, self.part = w, full, part
        self.g1, self.s1, self.g2, self.s2 = g1, s1, g2, s2
        self.send, self.recv = send, recv

    def over_col(self, i, src, dst):
        w = self.w
        for d in (8, 7, 9, 6, 10, 5, 11, 4, 12, 3, 13, 2, 14, 1, 15):
            to = (w.c + d) % NCOL
            rcopy(src(to), dst.at[w.c], self.send.at[i], self.recv.at[i], (w.r, to)).start()

    def over_row(self, i, src, dst):
        w = self.w
        for d in (4, 3, 5, 2, 6, 1, 7):
            to = (w.r + d) % NROW
            rcopy(src, dst.at[w.r], self.send.at[i], self.recv.at[i], (to, w.c)).start()

    def all_of(self, i, ref, count):
        part = ref.at[pl.ds(0, count - 1)]
        return rcopy(part, part, self.send.at[i], self.recv.at[i], (self.w.r, self.w.xc(1)))

    def phase1(self):
        w = self.w
        self.over_col(0, lambda to: self.part.at[to], self.g1)
        self.g1[w.c] = self.part[w.c]

    def phase2(self):
        w = self.w
        self.all_of(0, self.g1, NCOL).wait_recv()
        total = self.g1[0]
        for i in range(1, NCOL):
            total = total + self.g1[i]
        self.s1[...] = total
        self.over_row(1, self.s1, self.g2)
        self.g2[w.r] = total

    def phase3(self):
        w = self.w
        self.all_of(1, self.g2, NROW).wait_recv()
        total = self.g2[0]
        for i in range(1, NROW):
            total = total + self.g2[i]
        total = total * (1.0 / (2 * GROUP * NROW * NCOL))
        self.s2[...] = total
        self.over_col(2, lambda to: self.s2, self.full)
        self.full[w.c] = total

    def join(self):
        self.all_of(2, self.full, NCOL).wait_recv()

    def drain(self):
        for i, ref in enumerate((self.g1, self.g2, self.full)):
            self.all_of(i, ref, NROW if i == 1 else NCOL).wait_send()


GRAM_SCRATCH = [
    pltpu.VMEM((NCOL, 8, NV), F32),
    pltpu.VMEM((NCOL, 8, NV), F32),
    pltpu.VMEM((8, NV), F32),
    pltpu.VMEM((NROW, 8, NV), F32),
    pltpu.VMEM((8, NV), F32),
    pltpu.SemaphoreType.DMA((3,)),
    pltpu.SemaphoreType.DMA((3,)),
]
NG = len(GRAM_SCRATCH)
NR = len(RS_SCRATCH)


def self_product(v):
    return lax.dot_general(v, v, (((0,), (0,)), ((), ())), precision=HIGH, preferred_element_type=F32)


def times_inverse(v, linv):
    return lax.dot_general(v, linv, (((1,), (1,)), ((), ())), precision=HIGH, preferred_element_type=F32)


def eliminate(gram, first, last):
    lane = lax.broadcasted_iota(jnp.int32, (8, NV), 1)
    sub = lax.broadcasted_iota(jnp.int32, (8, NV), 0)
    row = lax.broadcasted_iota(jnp.int32, (NV, NV), 0)
    inside = lax.broadcasted_iota(jnp.int32, (NV, NV), 1) < 8
    def block(it, w):
        top = w[:8]
        cols = [jnp.broadcast_to(w[:, i:i+1], (NV, NV)) for i in range(8)]
        b = [c[:8] for c in cols]
        x = jnp.where(lane < 8, jnp.where(lane == sub, 1.0, 0.0), top)
        fin = x
        for j in range(8):
            here = sub == j
            p = jnp.broadcast_to(b[j][j:j+1], (8, NV))
            inv = 1.0 / p
            xr = jnp.broadcast_to(x[j:j+1], (8, NV))
            fin = jnp.where(here, xr * (1.0 / jnp.sqrt(p)), fin)
            xs = xr * inv
            cj = b[j]
            x = jnp.where(here, xs, x - cj * xs)
            for k in range(j + 1, 8):
                bs = jnp.broadcast_to(b[k][j:j+1], (8, NV)) * inv
                b[k] = jnp.where(here, bs, b[k] - cj * bs)
        upd = jnp.where(inside, 0.0, w)
        for i in range(8):
            upd = upd - cols[i] * jnp.broadcast_to(x[i:i+1], (NV, NV))
        w = jnp.where(row < NV - 8 * it, upd, w)
        w = jnp.concatenate([w[8:], fin], axis=0)
        return pltpu.roll(w, NV - 8, 1)
    return lax.fori_loop(first, last, block, gram)


def lower_part(w):
    row = lax.broadcasted_iota(jnp.int32, (NV, NV), 0)
    return jnp.where(lax.broadcasted_iota(jnp.int32, (NV, NV), 1) <= row, w, 0.0)


def split(v):
    hi = v.astype(BF16)
    lo = (v - hi.astype(F32)).astype(BF16)
    return hi, lo


def link_kernel(places, links, ends, last_row, last_col):
    listed = places.shape[1]
    for i in range(32):
        last_row[i] = 0
    for i in range(16):
        last_col[i] = 0
    for k in range(listed):
        r = places[0, k]
        c = places[1, k]
        links[0, k] = last_row[r]
        links[1, k] = last_col[c]
        last_row[r] = k + 1
        last_col[c] = k + 1
    for i in range(32):
        ends[0, i] = last_row[i]
    for i in range(16):
        ends[1, i] = last_col[i]


class Tile:
    def __init__(self, places, links, ends, blocks, sem, flat, chain, wcol, xrow):
        self.places, self.links, self.ends, self.blocks, self.sem = places, links, ends, blocks, sem
        self.flat, self.chain, self.wcol, self.xrow = flat, chain, wcol, xrow
        self.steps = blocks.shape[0] // CHUNK

    def piece(self, i):
        return pltpu.make_async_copy(
            self.blocks.at[pl.ds(i * CHUNK, CHUNK)],
            self.chain.at[pl.ds(i * CHUNK + 1, CHUNK)],
            self.sem.at[i],
        )

    def fetch(self):
        for i in range(self.steps):
            self.piece(i).start()

    def convert(self, lo, hi):
        for i in range(lo, hi):
            self.piece(i).wait()

            def one(k, carry):
                hi_part, lo_part = split(self.chain[i * CHUNK + 1 + k])
                self.flat[i * CHUNK + k] = jnp.concatenate([hi_part, lo_part], axis=1)
                return carry

            lax.fori_loop(0, CHUNK, one, 0, unroll=CHUNK)

    def clear(self):
        self.chain[0] = jnp.zeros((BLK, BLK), F32)

    def take_cols(self, colbuf):
        def one(i, carry):
            hi, lo = split(colbuf[i])
            for h in (0, 1):
                a, b = hi[h * BLK : (h + 1) * BLK], lo[h * BLK : (h + 1) * BLK]
                self.wcol[2 * i + h] = jnp.concatenate([jnp.concatenate([a, b], axis=1)] * 2, axis=0)
            return carry

        lax.fori_loop(0, NROW, one, 0, unroll=4)

    def take_rows(self, rowbuf):
        def one(i, carry):
            hi, lo = split(rowbuf[i].T)
            for h in (0, 1):
                a, b = hi[:, h * BLK : (h + 1) * BLK], lo[:, h * BLK : (h + 1) * BLK]
                self.xrow[2 * i + h] = jnp.concatenate([a, b], axis=1)
            return carry

        lax.fori_loop(0, NCOL, one, 0, unroll=4)

    def direct(self, lo, hi):
        def step(i, carry):
            for b in range(CHUNK):
                k = i * CHUNK + b
                d = jnp.dot(self.flat[k], self.wcol[self.places[1, k]], preferred_element_type=F32)
                self.chain[k + 1] = d[:, :NV] + d[:, NV:] + self.chain[self.links[0, k]]
            return carry

        lax.fori_loop(lo, hi, step, 0)

    def summed(self, rows):
        def out(i, carry):
            for h in (0, 1):
                rows[i, pl.ds(h * BLK, BLK)] = self.chain[self.ends[0, 2 * i + h]]
            return carry

        lax.fori_loop(0, NCOL, out, 0, unroll=4)

    def flip(self, lo, hi):
        def step(i, carry):
            for b in range(CHUNK):
                k = i * CHUNK + b
                flat = self.flat[k]
                e = jnp.dot(
                    self.xrow[self.places[0, k]],
                    jnp.concatenate([flat, flat], axis=0),
                    preferred_element_type=F32,
                )
                self.chain[k + 1] = e[:, :BLK] + e[:, BLK:] + self.chain[self.links[1, k]]
            return carry

        lax.fori_loop(lo, hi, step, 0)

    def flipped(self, cols):
        def out(i, carry):
            for h in (0, 1):
                cols[i, pl.ds(h * BLK, BLK)] = self.chain[self.ends[1, 2 * i + h]].T
            return carry

        lax.fori_loop(0, NROW, out, 0, unroll=4)


APP_SCRATCH = (
    [pltpu.VMEM((NCOL, GROUP, NV), F32), pltpu.VMEM((NROW, GROUP, NV), F32)]
    + GATHER_SEMS
    + RS_SCRATCH
    + [pltpu.VMEM((NCOL, 8, NV), F32)]
    + GRAM_SCRATCH
)
NA = len(APP_SCRATCH)


def whole_kernel(
    places, links, ends, blocks, vec, out, sem, flat, chain, wcol, xrow, rows, cols, pool1, pool2, pool3, work, *scratch
):
    w = Where()
    tile = Tile(places, links, ends, blocks, sem, flat, chain, wcol, xrow)
    n = tile.steps
    tile.fetch()
    entry_barrier(w.neighbours())
    posts1, posts2, posts3 = Posts(pool1), Posts(pool2), Posts(pool3)

    class App:
        def __init__(self, refs, up, lo, gather_posts, scatter_posts):
            self.rowbuf, self.colbuf = refs[:2]
            at = 2 + NS
            self.full = refs[at + NR]
            self.part = refs[at + NR + 1]
            self.g = Gather(w, gather_posts, up, lo, self.rowbuf, self.colbuf, *refs[2:at])
            self.s = Scatter(w, scatter_posts, rows, cols, refs[at : at + NR])
            self.gram = GramSum(w, self.full, *refs[at + NR + 1 :])

    one = App(scratch[:NA], vec.at[0], vec.at[1], posts1, posts1)
    two = App(scratch[NA : 2 * NA], out.at[0], out.at[1], posts2, posts3)

    g, s = one.g, one.s
    g.start_y_u()
    g.start_y_l()
    g.start_l()
    g.start_u()
    tile.clear()
    tile.convert(0, 3)
    g.from_y_l()
    g.from_y_u()
    tile.convert(3, 6)
    g.from_x(False)
    tile.convert(6, n)
    g.rest_l()
    tile.take_cols(one.colbuf)
    tile.direct(0, 3)
    g.from_x(True, (1,))
    tile.direct(3, 6)
    g.from_x(True, (3, 2))
    tile.direct(6, n)
    tile.summed(rows)
    s.siblings()
    g.rest_u()
    tile.take_rows(one.rowbuf)
    tile.flip(0, 3)
    s.far_x()
    tile.flip(3, 6)
    s.join(4, 5)
    s.x.through(1)
    s.x.near(0)
    tile.flip(6, n)
    s.join(6, 7)
    s.x.through(0)
    tile.flipped(cols)
    s.far_z()
    s.to_y_x()
    s.z.through(1)
    s.z.near(0)
    s.z.through(0)
    s.own(1, s.x)
    out[0] = s.final(1) * LIFT
    g = two.g
    g.start_y_u()
    g.start_u()
    s.to_y_z()
    part = self_product(out[0])
    s.own(0, s.z)
    out[1] = s.final(0) * LIFT
    g.start_y_l()
    g.start_l()
    one.part[...] = (part + self_product(out[1])).reshape(NCOL, 8, NV)
    one.gram.phase1()

    s = two.s
    g.from_y_u()
    g.from_x(False)
    g.from_y_l()
    one.gram.phase2()
    g.from_x(True)
    g.rest_u()
    tile.take_rows(two.rowbuf)
    tile.flip(0, n // 2)
    one.gram.phase3()
    tile.flip(n // 2, n)
    posts1.drain()
    tile.flipped(cols)
    s.far_z()
    g.rest_l()
    tile.take_cols(two.colbuf)
    tile.direct(0, n // 2)
    s.z.through(1)
    s.z.near(0)
    tile.direct(n // 2, n)
    s.z.through(0)
    tile.summed(rows)
    s.siblings()
    one.gram.join()
    one.gram.drain()
    work[...] = eliminate(one.full[...].reshape(NV, NV), 0, 4)
    s.far_x()
    s.join(4, 5)
    work[...] = eliminate(work[...], 4, 8)
    s.x.through(1)
    s.x.near(0)
    s.join(6, 7)
    s.x.through(0)
    s.to_y_z()
    work[...] = eliminate(work[...], 8, 12)
    s.own(0, s.z)
    s.to_y_x()
    work[...] = lower_part(eliminate(work[...], 12, 16))
    posts2.drain()
    out[1] = times_inverse(s.final(0), work[...])
    part = self_product(out[1])
    s.own(1, s.x)
    out[0] = times_inverse(s.final(1), work[...])
    two.part[...] = (part + self_product(out[0])).reshape(NCOL, 8, NV)
    two.gram.phase1()
    two.gram.phase2()
    two.gram.phase3()
    two.gram.join()
    linv = lower_part(eliminate(two.full[...].reshape(NV, NV), 0, 16))
    two.gram.drain()
    posts3.drain()
    out[0] = times_inverse(out[0], linv)
    out[1] = times_inverse(out[1], linv)


def local(blocks, coords, vectors):
    values = blocks.reshape(blocks.shape[2], BLK, BLK)
    places = coords.reshape(2, coords.shape[3])
    listed = values.shape[0]
    scalars = pl.BlockSpec(memory_space=pltpu.SMEM)
    links, ends = pl.pallas_call(
        link_kernel,
        out_shape=(
            jax.ShapeDtypeStruct((2, listed), jnp.int32),
            jax.ShapeDtypeStruct((2, 32), jnp.int32),
        ),
        in_specs=[scalars],
        out_specs=(scalars, scalars),
        scratch_shapes=[pltpu.SMEM((32,), jnp.int32), pltpu.SMEM((16,), jnp.int32)],
        name="links",
    )(places)
    return pl.pallas_call(
        whole_kernel,
        out_shape=jax.ShapeDtypeStruct((2, GROUP, NV), F32),
        in_specs=[scalars] * 3 + [pl.BlockSpec(memory_space=pl.ANY), VM],
        out_specs=VM,
        scratch_shapes=[
            pltpu.SemaphoreType.DMA((listed // CHUNK,)),
            pltpu.VMEM((listed, BLK, 2 * BLK), BF16),
            pltpu.VMEM((listed + 1, BLK, BLK), F32),
            pltpu.VMEM((16, 2 * BLK, 2 * NV), BF16),
            pltpu.VMEM((32, NV, 2 * BLK), BF16),
            pltpu.VMEM((NCOL, GROUP, NV), F32),
            pltpu.VMEM((NROW, GROUP, NV), F32),
        ]
        + POOLS
        + [pltpu.VMEM((NV, NV), F32)]
        + APP_SCRATCH
        + APP_SCRATCH,
        compiler_params=pltpu.CompilerParams(
            collective_id=0, has_side_effects=True, vmem_limit_bytes=56 << 20
        ),
        name="whole",
    )(places, links, ends, values, vectors)


def solution(mesh):
    return jax.shard_map(
        local,
        mesh=mesh,
        in_specs=(
            P("row", "col", None, None, None),
            P("row", "col", None, None),
            P(None, ("row", "col"), None),
        ),
        out_specs=P(None, ("row", "col"), None),
        check_vma=False,
    )
```

```python
import functools

import jax
import jax.numpy as jnp
from jax import lax
from jax.experimental import pallas as pl
from jax.experimental.pallas import tpu as pltpu
from jax.sharding import PartitionSpec as P

MESH = pl.DeviceIdType.MESH
HIGH = lax.Precision.HIGHEST
F32 = jnp.float32
BF16 = jnp.bfloat16

GROUP = 256
NV = 128
BLK = 128
NROW = 8
NCOL = 16
CHUNK = 17
VM = pl.BlockSpec(memory_space=pltpu.VMEM)
LIFT = 2.0**20


class Where:
    def __init__(self):
        self.r = lax.axis_index("row")
        self.c = lax.axis_index("col")
        self.z = self.r // 2
        self.yl = self.r % 2
        self.yh = self.c // 8
        self.x = (self.c // 2) % 4
        self.core = self.c % 2

    def zr(self, dz, other=False):
        yl = 1 - self.yl if other else self.yl
        return ((self.z + dz) % 4) * 2 + yl

    def xc(self, dx, other_y=False, other_core=False):
        yh = 1 - self.yh if other_y else self.yh
        core = 1 - self.core if other_core else self.core
        return (yh * 4 + (self.x + dx) % 4) * 2 + core

    def neighbours(self):
        out = [(self.zr(dz), self.c) for dz in (1, 2, 3)]
        out.append((self.zr(0, True), self.c))
        out += [(self.r, self.xc(dx)) for dx in (1, 2, 3)]
        out.append((self.r, self.xc(0, True)))
        out.append((self.r, self.xc(0, False, True)))
        return out


def entry_barrier(partners):
    barrier = pltpu.get_barrier_semaphore()
    for p in partners:
        pl.semaphore_signal(barrier, inc=1, device_id=p, device_id_type=MESH)
    pl.semaphore_wait(barrier, len(partners))


def rcopy(src, dst, send, recv, dev):
    return pltpu.make_async_remote_copy(
        src_ref=src,
        dst_ref=dst,
        send_sem=send,
        recv_sem=recv,
        device_id=dev,
        device_id_type=MESH,
    )


HALF = GROUP // 2


def half(ref, h):
    return ref.at[pl.ds(h * HALF, HALF)]


class Posts:
    def __init__(self, pool):
        self.pool = pool
        self.sent = []
        self.oldest = 0

    def post(self, src, dst, recv, dev):
        slots = self.pool.shape[0]
        if len(self.sent) - self.oldest == slots:
            self.sent[self.oldest].wait_send()
            self.oldest += 1
        cp = rcopy(src, dst, self.pool.at[len(self.sent) % slots], recv, dev)
        cp.start()
        self.sent.append(cp)
        return cp

    def arrived(self, ref, recv, dev):
        rcopy(ref, ref, self.pool.at[0], recv, dev).wait_recv()

    def drain(self):
        for cp in self.sent[self.oldest :]:
            cp.wait_send()
        self.oldest = len(self.sent)


class Gather:
    def __init__(self, w, posts, up, lo, rowbuf, colbuf, r_u, r_sib, r_y, r_l):
        self.w, self.posts, self.up, self.lo = w, posts, up, lo
        self.rowbuf, self.colbuf = rowbuf, colbuf
        self.r_u, self.r_sib, self.r_y, self.r_l = r_u, r_sib.at[0], r_y.at[0], r_l.at[0]
        self.sibling = (w.r, w.xc(0, False, True))

    def send_u(self, src, p, dev):
        self.posts.post(src, self.rowbuf.at[p], self.r_u.at[p // 2], dev)

    def to_sibling(self, src, p):
        self.posts.post(src, self.rowbuf.at[p], self.r_sib, self.sibling)

    def send_l(self, src, q, recv, dev):
        self.posts.post(src, self.colbuf.at[q], recv, dev)

    def wait_u(self, p):
        self.posts.arrived(self.rowbuf.at[p], self.r_u.at[p // 2], self.sibling)

    def start_y_l(self):
        self.send_l(self.lo, self.w.r, self.r_y, (self.w.zr(0, True), self.w.c))

    def start_y_u(self):
        self.send_u(self.up, self.w.c, (self.w.r, self.w.xc(0, True)))

    def start_l(self):
        w = self.w
        for d in (2, 1, 3):
            self.send_l(self.lo, w.r, self.r_l, (w.zr(d), w.c))
        self.colbuf[w.r] = self.lo[...]

    def start_u(self):
        w = self.w
        for d in (2, 1, 3):
            self.send_u(self.up, w.c, (w.r, w.xc(d)))
        self.to_sibling(self.up, w.c)
        self.rowbuf[w.c] = self.up[...]

    def from_y_l(self):
        w = self.w
        q = w.zr(0, True)
        self.posts.arrived(self.colbuf.at[q], self.r_y, self.sibling)
        for d in (2, 1, 3):
            self.send_l(self.colbuf.at[q], q, self.r_l, (w.zr(d), w.c))

    def from_y_u(self):
        w = self.w
        p = w.xc(0, True)
        self.wait_u(p)
        for d in (2, 1, 3):
            self.send_u(self.rowbuf.at[p], p, (w.r, w.xc(d)))
        self.to_sibling(self.rowbuf.at[p], p)

    def from_x(self, other, steps=(1, 3, 2)):
        for d in steps:
            p = self.w.xc(d, other)
            self.wait_u(p)
            self.to_sibling(self.rowbuf.at[p], p)

    def rest_l(self):
        self.posts.arrived(self.colbuf.at[pl.ds(0, 6)], self.r_l, self.sibling)

    def rest_u(self):
        self.posts.arrived(self.rowbuf.at[pl.ds(0, 8)], self.r_sib, self.sibling)


GATHER_SEMS = [pltpu.SemaphoreType.DMA((n,)) for n in (8, 1, 1, 1)]
NS = len(GATHER_SEMS)


class Ring:
    def __init__(self, posts, dev, part, dep, rel, fin, r_rel, r_fin):
        self.posts, self.dev, self.part = posts, dev, part
        self.dep, self.rel, self.fin = dep, rel, fin
        self.r_rel, self.r_fin = r_rel, r_fin

    def far(self, o):
        for k, s in enumerate((1, -1)):
            self.posts.post(half(self.part(2, o), k), self.rel.at[o, k], self.r_rel.at[o], self.dev(s))

    def near(self, o):
        for k, s in enumerate((1, -1)):
            h = 1 - k
            self.posts.post(half(self.part(s, o), h), half(self.fin.at[o, k], h), self.r_fin.at[o], self.dev(s))

    def through(self, o):
        self.posts.arrived(self.rel.at[o], self.r_rel.at[o], self.dev(1))
        for k, s in enumerate((1, -1)):
            self.dep[o, k] = half(self.part(s, o), k)[...] + self.rel[o, k]
            self.posts.post(self.dep.at[o, k], half(self.fin.at[o, k], k), self.r_fin.at[o], self.dev(s))

    def total(self, o):
        self.posts.arrived(self.fin.at[o], self.r_fin.at[o], self.dev(1))
        return self.part(0, o)[...] + self.fin[o, 0] + self.fin[o, 1]


class Scatter:
    SLOTS = [(2, 1), (1, 1), (3, 1), (2, 0), (1, 0), (3, 0), (0, 1), (0, 0)]

    def __init__(self, w, posts, rows, cols, scratch):
        self.acc, self.sib, self.r_sib = scratch[:3]
        x, z = scratch[3:8], scratch[8:13]
        self.mid, self.ybuf, self.r_y = scratch[13:]
        self.w, self.posts, self.rows = w, posts, rows
        self.sibling = (w.r, w.xc(0, False, True))
        at = {slot: i for i, slot in enumerate(self.SLOTS)}
        self.x = Ring(posts, lambda s: (w.r, w.xc(s % 4)), lambda d, o: self.acc.at[at[d % 4, o]], *x)
        self.z = Ring(posts, lambda s: (w.zr(s % 4), w.c), lambda d, o: cols.at[w.zr(d % 4, o == 1)], *z)

    def siblings(self):
        for i, (d, o) in enumerate(self.SLOTS):
            src = self.rows.at[self.w.xc(d, o == 1, True)]
            self.posts.post(src, self.sib.at[i], self.r_sib.at[i], self.sibling)

    def join(self, *ids):
        for i in ids:
            self.posts.arrived(self.sib.at[i], self.r_sib.at[i], self.sibling)
            d, o = self.SLOTS[i]
            self.acc[i] = self.rows[self.w.xc(d, o == 1)] + self.sib[i]

    def far_x(self):
        self.join(0)
        self.x.far(1)
        self.join(1, 2)
        self.x.near(1)
        self.join(3)
        self.x.far(0)

    def far_z(self):
        self.z.far(1)
        self.z.near(1)
        self.z.far(0)

    def to_y(self, j, dev, value):
        self.mid[j] = value
        self.posts.post(self.mid.at[j], self.ybuf.at[j], self.r_y.at[j], dev)

    def to_y_x(self):
        self.to_y(1, (self.w.r, self.w.xc(0, True)), self.x.total(1))

    def to_y_z(self):
        self.to_y(0, (self.w.zr(0, True), self.w.c), self.z.total(1))

    def own(self, j, ring):
        self.mid[2 + j] = ring.total(0)

    def final(self, j):
        self.posts.arrived(self.ybuf.at[j], self.r_y.at[j], self.sibling)
        return self.mid[2 + j] + self.ybuf[j]


RING_SCRATCH = [
    pltpu.VMEM((2, 2, HALF, NV), F32),
    pltpu.VMEM((2, 2, HALF, NV), F32),
    pltpu.VMEM((2, 2, GROUP, NV), F32),
    pltpu.SemaphoreType.DMA((2,)),
    pltpu.SemaphoreType.DMA((2,)),
]
RS_SCRATCH = (
    [
        pltpu.VMEM((8, GROUP, NV), F32),
        pltpu.VMEM((8, GROUP, NV), F32),
        pltpu.SemaphoreType.DMA((8,)),
    ]
    + RING_SCRATCH
    + RING_SCRATCH
    + [
        pltpu.VMEM((4, GROUP, NV), F32),
        pltpu.VMEM((2, GROUP, NV), F32),
        pltpu.SemaphoreType.DMA((2,)),
    ]
)
POOLS = [pltpu.SemaphoreType.DMA((n,)) for n in (34, 22, 34)]


class GramSum:
    def __init__(self, w, full, part, g1, s1, g2, s2, send, recv):
        self.w, self.full, self.part = w, full, part
        self.g1, self.s1, self.g2, self.s2 = g1, s1, g2, s2
        self.send, self.recv = send, recv

    def over_col(self, i, src, dst):
        w = self.w
        for d in (8, 7, 9, 6, 10, 5, 11, 4, 12, 3, 13, 2, 14, 1, 15):
            to = (w.c + d) % NCOL
            rcopy(src(to), dst.at[w.c], self.send.at[i], self.recv.at[i], (w.r, to)).start()

    def over_row(self, i, src, dst):
        w = self.w
        for d in (4, 3, 5, 2, 6, 1, 7):
            to = (w.r + d) % NROW
            rcopy(src, dst.at[w.r], self.send.at[i], self.recv.at[i], (to, w.c)).start()

    def all_of(self, i, ref, count):
        part = ref.at[pl.ds(0, count - 1)]
        return rcopy(part, part, self.send.at[i], self.recv.at[i], (self.w.r, self.w.xc(1)))

    def phase1(self):
        w = self.w
        self.over_col(0, lambda to: self.part.at[to], self.g1)
        self.g1[w.c] = self.part[w.c]

    def phase2(self):
        w = self.w
        self.all_of(0, self.g1, NCOL).wait_recv()
        total = self.g1[0]
        for i in range(1, NCOL):
            total = total + self.g1[i]
        self.s1[...] = total
        self.over_row(1, self.s1, self.g2)
        self.g2[w.r] = total

    def phase3(self):
        w = self.w
        self.all_of(1, self.g2, NROW).wait_recv()
        total = self.g2[0]
        for i in range(1, NROW):
            total = total + self.g2[i]
        total = total * (1.0 / (2 * GROUP * NROW * NCOL))
        self.s2[...] = total
        self.over_col(2, lambda to: self.s2, self.full)
        self.full[w.c] = total

    def join(self):
        self.all_of(2, self.full, NCOL).wait_recv()

    def drain(self):
        for i, ref in enumerate((self.g1, self.g2, self.full)):
            self.all_of(i, ref, NROW if i == 1 else NCOL).wait_send()


GRAM_SCRATCH = [
    pltpu.VMEM((NCOL, 8, NV), F32),
    pltpu.VMEM((NCOL, 8, NV), F32),
    pltpu.VMEM((8, NV), F32),
    pltpu.VMEM((NROW, 8, NV), F32),
    pltpu.VMEM((8, NV), F32),
    pltpu.SemaphoreType.DMA((3,)),
    pltpu.SemaphoreType.DMA((3,)),
]
NG = len(GRAM_SCRATCH)
NR = len(RS_SCRATCH)


def self_product(v):
    return lax.dot_general(v, v, (((0,), (0,)), ((), ())), precision=HIGH, preferred_element_type=F32)


def times_inverse(v, linv):
    return lax.dot_general(v, linv, (((1,), (1,)), ((), ())), precision=HIGH, preferred_element_type=F32)


def eliminate(gram, first, last):
    lane = lax.broadcasted_iota(jnp.int32, (8, NV), 1)
    sub = lax.broadcasted_iota(jnp.int32, (8, NV), 0)
    row = lax.broadcasted_iota(jnp.int32, (NV, NV), 0)
    inside = lax.broadcasted_iota(jnp.int32, (NV, NV), 1) < 8
    def block(it, w):
        top = w[:8]
        cols = [jnp.broadcast_to(w[:, i:i+1], (NV, NV)) for i in range(8)]
        b = [c[:8] for c in cols]
        x = jnp.where(lane < 8, jnp.where(lane == sub, 1.0, 0.0), top)
        fin = x
        for j in range(8):
            here = sub == j
            p = jnp.broadcast_to(b[j][j:j+1], (8, NV))
            inv = 1.0 / p
            xr = jnp.broadcast_to(x[j:j+1], (8, NV))
            fin = jnp.where(here, xr * (1.0 / jnp.sqrt(p)), fin)
            xs = xr * inv
            cj = b[j]
            x = jnp.where(here, xs, x - cj * xs)
            for k in range(j + 1, 8):
                bs = jnp.broadcast_to(b[k][j:j+1], (8, NV)) * inv
                b[k] = jnp.where(here, bs, b[k] - cj * bs)
        upd = jnp.where(inside, 0.0, w)
        for i in range(8):
            upd = upd - cols[i] * jnp.broadcast_to(x[i:i+1], (NV, NV))
        w = jnp.where(row < NV - 8 * it, upd, w)
        w = jnp.concatenate([w[8:], fin], axis=0)
        return pltpu.roll(w, NV - 8, 1)
    return lax.fori_loop(first, last, block, gram)


def lower_part(w):
    row = lax.broadcasted_iota(jnp.int32, (NV, NV), 0)
    return jnp.where(lax.broadcasted_iota(jnp.int32, (NV, NV), 1) <= row, w, 0.0)


def split(v):
    hi = v.astype(BF16)
    lo = (v - hi.astype(F32)).astype(BF16)
    return hi, lo


def link_tables(coords, links, ends):
    listed = coords.shape[1]
    lane = lax.broadcasted_iota(jnp.int32, (listed, listed), 1)
    sub = lax.broadcasted_iota(jnp.int32, (listed, listed), 0)
    count = lax.broadcasted_iota(jnp.int32, (listed, NV), 0) + 1
    place = lax.broadcasted_iota(jnp.int32, (listed, NV), 1)
    links[...] = jnp.zeros(links.shape, jnp.int32)
    ends[...] = jnp.zeros(ends.shape, jnp.int32)
    for t in (0, 1):
        along = jnp.broadcast_to(coords[t : t + 1, :], (listed, listed))
        down = jnp.max(jnp.where(lane == sub, along, 0), axis=1, keepdims=True)
        before = jnp.logical_and(jnp.broadcast_to(down, (listed, listed)) == along, sub < lane)
        links[t : t + 1, :listed] = jnp.max(jnp.where(before, sub + 1, 0), axis=0, keepdims=True)
        here = jnp.broadcast_to(down, (listed, NV)) == place
        ends[t : t + 1, :] = jnp.max(jnp.where(here, count, 0), axis=0, keepdims=True)


class Tile:
    def __init__(self, places, links, ends, blocks, sem, flat, chain, wcol, xrow):
        self.places, self.links, self.ends, self.blocks, self.sem = places, links, ends, blocks, sem
        self.flat, self.chain, self.wcol, self.xrow = flat, chain, wcol, xrow
        self.steps = blocks.shape[0] // CHUNK

    def piece(self, i):
        return pltpu.make_async_copy(
            self.blocks.at[pl.ds(i * CHUNK, CHUNK)],
            self.chain.at[pl.ds(i * CHUNK + 1, CHUNK)],
            self.sem.at[i],
        )

    def fetch(self):
        for i in range(self.steps):
            self.piece(i).start()

    def convert(self, lo, hi):
        for i in range(lo, hi):
            self.piece(i).wait()

            def one(k, carry):
                hi_part, lo_part = split(self.chain[i * CHUNK + 1 + k])
                self.flat[i * CHUNK + k] = jnp.concatenate([hi_part, lo_part], axis=1)
                return carry

            lax.fori_loop(0, CHUNK, one, 0, unroll=CHUNK)

    def clear(self):
        self.chain[0] = jnp.zeros((BLK, BLK), F32)

    def take_cols(self, colbuf):
        def one(i, carry):
            hi, lo = split(colbuf[i])
            for h in (0, 1):
                a, b = hi[h * BLK : (h + 1) * BLK], lo[h * BLK : (h + 1) * BLK]
                self.wcol[2 * i + h] = jnp.concatenate([jnp.concatenate([a, b], axis=1)] * 2, axis=0)
            return carry

        lax.fori_loop(0, NROW, one, 0, unroll=4)

    def take_rows(self, rowbuf):
        def one(i, carry):
            hi, lo = split(rowbuf[i].T)
            for h in (0, 1):
                a, b = hi[:, h * BLK : (h + 1) * BLK], lo[:, h * BLK : (h + 1) * BLK]
                self.xrow[2 * i + h] = jnp.concatenate([a, b], axis=1)
            return carry

        lax.fori_loop(0, NCOL, one, 0, unroll=4)

    def direct(self, lo, hi):
        def step(i, carry):
            for b in range(CHUNK):
                k = i * CHUNK + b
                d = jnp.dot(self.flat[k], self.wcol[self.places[1, k]], preferred_element_type=F32)
                self.chain[k + 1] = d[:, :NV] + d[:, NV:] + self.chain[self.links[0, k]]
            return carry

        lax.fori_loop(lo, hi, step, 0)

    def summed(self, rows):
        def out(i, carry):
            for h in (0, 1):
                rows[i, pl.ds(h * BLK, BLK)] = self.chain[self.ends[0, 2 * i + h]]
            return carry

        lax.fori_loop(0, NCOL, out, 0, unroll=4)

    def flip(self, lo, hi):
        def step(i, carry):
            for b in range(CHUNK):
                k = i * CHUNK + b
                flat = self.flat[k]
                e = jnp.dot(
                    self.xrow[self.places[0, k]],
                    jnp.concatenate([flat, flat], axis=0),
                    preferred_element_type=F32,
                )
                self.chain[k + 1] = e[:, :BLK] + e[:, BLK:] + self.chain[self.links[1, k]]
            return carry

        lax.fori_loop(lo, hi, step, 0)

    def flipped(self, cols):
        def out(i, carry):
            for h in (0, 1):
                cols[i, pl.ds(h * BLK, BLK)] = self.chain[self.ends[1, 2 * i + h]].T
            return carry

        lax.fori_loop(0, NROW, out, 0, unroll=4)


APP_SCRATCH = (
    [pltpu.VMEM((NCOL, GROUP, NV), F32), pltpu.VMEM((NROW, GROUP, NV), F32)]
    + GATHER_SEMS
    + RS_SCRATCH
    + [pltpu.VMEM((NCOL, 8, NV), F32)]
    + GRAM_SCRATCH
)
NA = len(APP_SCRATCH)


def whole_kernel(
    places, coords, blocks, vec, out, links, ends, vlinks, vends, s_tab, sem, flat, chain, wcol, xrow, rows, cols, pool1, pool2, pool3, work, *scratch
):
    w = Where()
    tile = Tile(places, links, ends, blocks, sem, flat, chain, wcol, xrow)
    n = tile.steps
    tile.fetch()
    entry_barrier(w.neighbours())
    posts1, posts2, posts3 = Posts(pool1), Posts(pool2), Posts(pool3)

    class App:
        def __init__(self, refs, up, lo, gather_posts, scatter_posts):
            self.rowbuf, self.colbuf = refs[:2]
            at = 2 + NS
            self.full = refs[at + NR]
            self.part = refs[at + NR + 1]
            self.g = Gather(w, gather_posts, up, lo, self.rowbuf, self.colbuf, *refs[2:at])
            self.s = Scatter(w, scatter_posts, rows, cols, refs[at : at + NR])
            self.gram = GramSum(w, self.full, *refs[at + NR + 1 :])

    one = App(scratch[:NA], vec.at[0], vec.at[1], posts1, posts1)
    two = App(scratch[NA : 2 * NA], out.at[0], out.at[1], posts2, posts3)

    g, s = one.g, one.s
    g.start_y_l()
    g.start_y_u()
    g.start_l()
    g.start_u()
    link_tables(coords, vlinks, vends)
    tables = [
        pltpu.make_async_copy(vlinks, links, s_tab.at[0]),
        pltpu.make_async_copy(vends, ends, s_tab.at[1]),
    ]
    for t in tables:
        t.start()
    tile.clear()
    tile.convert(0, 3)
    g.from_y_l()
    g.from_y_u()
    tile.convert(3, 6)
    g.from_x(False)
    tile.convert(6, n)
    for t in tables:
        t.wait()
    g.rest_l()
    tile.take_cols(one.colbuf)
    tile.direct(0, 3)
    g.from_x(True, (1,))
    tile.direct(3, 6)
    g.from_x(True, (3, 2))
    tile.direct(6, n)
    tile.summed(rows)
    s.siblings()
    g.rest_u()
    tile.take_rows(one.rowbuf)
    tile.flip(0, 3)
    s.far_x()
    tile.flip(3, 6)
    s.join(4, 5)
    s.x.through(1)
    s.x.near(0)
    tile.flip(6, n)
    s.join(6, 7)
    s.x.through(0)
    tile.flipped(cols)
    s.far_z()
    s.to_y_x()
    s.z.through(1)
    s.z.near(0)
    s.z.through(0)
    s.own(1, s.x)
    out[0] = s.final(1) * LIFT
    g = two.g
    g.start_y_u()
    g.start_u()
    s.to_y_z()
    part = self_product(out[0])
    s.own(0, s.z)
    out[1] = s.final(0) * LIFT
    g.start_y_l()
    g.start_l()
    one.part[...] = (part + self_product(out[1])).reshape(NCOL, 8, NV)
    one.gram.phase1()

    s = two.s
    g.from_y_u()
    g.from_x(False)
    g.from_y_l()
    one.gram.phase2()
    g.from_x(True)
    g.rest_u()
    tile.take_rows(two.rowbuf)
    tile.flip(0, n // 2)
    one.gram.phase3()
    tile.flip(n // 2, n)
    posts1.drain()
    tile.flipped(cols)
    s.far_z()
    g.rest_l()
    tile.take_cols(two.colbuf)
    tile.direct(0, n // 2)
    s.z.through(1)
    s.z.near(0)
    tile.direct(n // 2, n)
    s.z.through(0)
    tile.summed(rows)
    s.siblings()
    s.far_x()
    s.join(4, 5)
    one.gram.join()
    one.gram.drain()
    work[...] = eliminate(one.full[...].reshape(NV, NV), 0, 4)
    s.x.through(1)
    s.x.near(0)
    s.join(6, 7)
    work[...] = eliminate(work[...], 4, 8)
    s.x.through(0)
    s.to_y_z()
    work[...] = eliminate(work[...], 8, 12)
    s.own(0, s.z)
    s.to_y_x()
    work[...] = lower_part(eliminate(work[...], 12, 16))
    posts2.drain()
    out[1] = times_inverse(s.final(0), work[...])
    part = self_product(out[1])
    s.own(1, s.x)
    out[0] = times_inverse(s.final(1), work[...])
    two.part[...] = (part + self_product(out[0])).reshape(NCOL, 8, NV)
    two.gram.phase1()
    two.gram.phase2()
    two.gram.phase3()
    two.gram.join()
    linv = lower_part(eliminate(two.full[...].reshape(NV, NV), 0, 16))
    two.gram.drain()
    posts3.drain()
    out[0] = times_inverse(out[0], linv)
    out[1] = times_inverse(out[1], linv)


def local(blocks, coords, vectors):
    values = blocks.reshape(blocks.shape[2], BLK, BLK)
    places = coords.reshape(2, coords.shape[3])
    listed = values.shape[0]
    scalars = pl.BlockSpec(memory_space=pltpu.SMEM)
    return pl.pallas_call(
        whole_kernel,
        out_shape=jax.ShapeDtypeStruct((2, GROUP, NV), F32),
        in_specs=[scalars, VM, pl.BlockSpec(memory_space=pl.ANY), VM],
        out_specs=VM,
        scratch_shapes=[
            pltpu.SMEM((8, 256), jnp.int32),
            pltpu.SMEM((8, NV), jnp.int32),
            pltpu.VMEM((8, 256), jnp.int32),
            pltpu.VMEM((8, NV), jnp.int32),
            pltpu.SemaphoreType.DMA((2,)),
            pltpu.SemaphoreType.DMA((listed // CHUNK,)),
            pltpu.VMEM((listed, BLK, 2 * BLK), BF16),
            pltpu.VMEM((listed + 1, BLK, BLK), F32),
            pltpu.VMEM((16, 2 * BLK, 2 * NV), BF16),
            pltpu.VMEM((32, NV, 2 * BLK), BF16),
            pltpu.VMEM((NCOL, GROUP, NV), F32),
            pltpu.VMEM((NROW, GROUP, NV), F32),
        ]
        + POOLS
        + [pltpu.VMEM((NV, NV), F32)]
        + APP_SCRATCH
        + APP_SCRATCH,
        compiler_params=pltpu.CompilerParams(
            collective_id=0, has_side_effects=True, vmem_limit_bytes=56 << 20
        ),
        name="whole",
    )(places, places, values, vectors)


def solution(mesh):
    return jax.shard_map(
        local,
        mesh=mesh,
        in_specs=(
            P("row", "col", None, None, None),
            P("row", "col", None, None),
            P(None, ("row", "col"), None),
        ),
        out_specs=P(None, ("row", "col"), None),
        check_vma=False,
    )
```

```python
import functools

import jax
import jax.numpy as jnp
from jax import lax
from jax.experimental import pallas as pl
from jax.experimental.pallas import tpu as pltpu
from jax.sharding import PartitionSpec as P

MESH = pl.DeviceIdType.MESH
HIGH = lax.Precision.HIGHEST
F32 = jnp.float32
BF16 = jnp.bfloat16

GROUP = 256
NV = 128
BLK = 128
NROW = 8
NCOL = 16
CHUNK = 17
VM = pl.BlockSpec(memory_space=pltpu.VMEM)
LIFT = 2.0**20


class Where:
    def __init__(self):
        self.r = lax.axis_index("row")
        self.c = lax.axis_index("col")
        self.z = self.r // 2
        self.yl = self.r % 2
        self.yh = self.c // 8
        self.x = (self.c // 2) % 4
        self.core = self.c % 2

    def zr(self, dz, other=False):
        yl = 1 - self.yl if other else self.yl
        return ((self.z + dz) % 4) * 2 + yl

    def xc(self, dx, other_y=False, other_core=False):
        yh = 1 - self.yh if other_y else self.yh
        core = 1 - self.core if other_core else self.core
        return (yh * 4 + (self.x + dx) % 4) * 2 + core

    def neighbours(self):
        out = [(self.zr(dz), self.c) for dz in (1, 2, 3)]
        out.append((self.zr(0, True), self.c))
        out += [(self.r, self.xc(dx)) for dx in (1, 2, 3)]
        out.append((self.r, self.xc(0, True)))
        out.append((self.r, self.xc(0, False, True)))
        return out


def entry_barrier(partners):
    barrier = pltpu.get_barrier_semaphore()
    for p in partners:
        pl.semaphore_signal(barrier, inc=1, device_id=p, device_id_type=MESH)
    pl.semaphore_wait(barrier, len(partners))


def rcopy(src, dst, send, recv, dev):
    return pltpu.make_async_remote_copy(
        src_ref=src,
        dst_ref=dst,
        send_sem=send,
        recv_sem=recv,
        device_id=dev,
        device_id_type=MESH,
    )


HALF = GROUP // 2


def half(ref, h):
    return ref.at[pl.ds(h * HALF, HALF)]


class Posts:
    def __init__(self, pool):
        self.pool = pool
        self.sent = []
        self.oldest = 0

    def post(self, src, dst, recv, dev):
        slots = self.pool.shape[0]
        if len(self.sent) - self.oldest == slots:
            self.sent[self.oldest].wait_send()
            self.oldest += 1
        cp = rcopy(src, dst, self.pool.at[len(self.sent) % slots], recv, dev)
        cp.start()
        self.sent.append(cp)
        return cp

    def arrived(self, ref, recv, dev):
        rcopy(ref, ref, self.pool.at[0], recv, dev).wait_recv()

    def drain(self):
        for cp in self.sent[self.oldest :]:
            cp.wait_send()
        self.oldest = len(self.sent)


class Gather:
    def __init__(self, w, posts, up, lo, rowbuf, colbuf, r_u, r_sib, r_y, r_l):
        self.w, self.posts, self.up, self.lo = w, posts, up, lo
        self.rowbuf, self.colbuf = rowbuf, colbuf
        self.r_u, self.r_sib, self.r_y, self.r_l = r_u, r_sib.at[0], r_y.at[0], r_l.at[0]
        self.sibling = (w.r, w.xc(0, False, True))

    def send_u(self, src, p, dev):
        self.posts.post(src, self.rowbuf.at[p], self.r_u.at[p // 2], dev)

    def to_sibling(self, src, p):
        self.posts.post(src, self.rowbuf.at[p], self.r_sib, self.sibling)

    def send_l(self, src, q, recv, dev):
        self.posts.post(src, self.colbuf.at[q], recv, dev)

    def wait_u(self, p):
        self.posts.arrived(self.rowbuf.at[p], self.r_u.at[p // 2], self.sibling)

    def start_y_l(self):
        self.send_l(self.lo, self.w.r, self.r_y, (self.w.zr(0, True), self.w.c))

    def start_y_u(self):
        self.send_u(self.up, self.w.c, (self.w.r, self.w.xc(0, True)))

    def start_l(self):
        w = self.w
        for d in (2, 1, 3):
            self.send_l(self.lo, w.r, self.r_l, (w.zr(d), w.c))
        self.colbuf[w.r] = self.lo[...]

    def start_u(self):
        w = self.w
        for d in (2, 1, 3):
            self.send_u(self.up, w.c, (w.r, w.xc(d)))
        self.to_sibling(self.up, w.c)
        self.rowbuf[w.c] = self.up[...]

    def from_y_l(self):
        w = self.w
        q = w.zr(0, True)
        self.posts.arrived(self.colbuf.at[q], self.r_y, self.sibling)
        for d in (2, 1, 3):
            self.send_l(self.colbuf.at[q], q, self.r_l, (w.zr(d), w.c))

    def from_y_u(self):
        w = self.w
        p = w.xc(0, True)
        self.wait_u(p)
        for d in (2, 1, 3):
            self.send_u(self.rowbuf.at[p], p, (w.r, w.xc(d)))
        self.to_sibling(self.rowbuf.at[p], p)

    def from_x(self, other, steps=(1, 3, 2)):
        for d in steps:
            p = self.w.xc(d, other)
            self.wait_u(p)
            self.to_sibling(self.rowbuf.at[p], p)

    def rest_l(self):
        self.posts.arrived(self.colbuf.at[pl.ds(0, 6)], self.r_l, self.sibling)

    def rest_u(self):
        self.posts.arrived(self.rowbuf.at[pl.ds(0, 8)], self.r_sib, self.sibling)


GATHER_SEMS = [pltpu.SemaphoreType.DMA((n,)) for n in (8, 1, 1, 1)]
NS = len(GATHER_SEMS)


class Ring:
    def __init__(self, posts, dev, part, dep, rel, fin, r_rel, r_fin):
        self.posts, self.dev, self.part = posts, dev, part
        self.dep, self.rel, self.fin = dep, rel, fin
        self.r_rel, self.r_fin = r_rel, r_fin

    def far(self, o):
        for k, s in enumerate((1, -1)):
            self.posts.post(half(self.part(2, o), k), self.rel.at[o, k], self.r_rel.at[o], self.dev(s))

    def near(self, o):
        for k, s in enumerate((1, -1)):
            h = 1 - k
            self.posts.post(half(self.part(s, o), h), half(self.fin.at[o, k], h), self.r_fin.at[o], self.dev(s))

    def through(self, o):
        self.posts.arrived(self.rel.at[o], self.r_rel.at[o], self.dev(1))
        for k, s in enumerate((1, -1)):
            self.dep[o, k] = half(self.part(s, o), k)[...] + self.rel[o, k]
            self.posts.post(self.dep.at[o, k], half(self.fin.at[o, k], k), self.r_fin.at[o], self.dev(s))

    def total(self, o):
        self.posts.arrived(self.fin.at[o], self.r_fin.at[o], self.dev(1))
        return self.part(0, o)[...] + self.fin[o, 0] + self.fin[o, 1]


class Scatter:
    SLOTS = [(2, 1), (1, 1), (3, 1), (2, 0), (1, 0), (3, 0), (0, 1), (0, 0)]

    def __init__(self, w, posts, rows, cols, scratch):
        self.acc, self.sib, self.r_sib = scratch[:3]
        x, z = scratch[3:8], scratch[8:13]
        self.mid, self.ybuf, self.r_y = scratch[13:]
        self.w, self.posts, self.rows = w, posts, rows
        self.sibling = (w.r, w.xc(0, False, True))
        at = {slot: i for i, slot in enumerate(self.SLOTS)}
        self.x = Ring(posts, lambda s: (w.r, w.xc(s % 4)), lambda d, o: self.acc.at[at[d % 4, o]], *x)
        self.z = Ring(posts, lambda s: (w.zr(s % 4), w.c), lambda d, o: cols.at[w.zr(d % 4, o == 1)], *z)

    def siblings(self):
        for i, (d, o) in enumerate(self.SLOTS):
            src = self.rows.at[self.w.xc(d, o == 1, True)]
            self.posts.post(src, self.sib.at[i], self.r_sib.at[i], self.sibling)

    def join(self, *ids):
        for i in ids:
            self.posts.arrived(self.sib.at[i], self.r_sib.at[i], self.sibling)
            d, o = self.SLOTS[i]
            self.acc[i] = self.rows[self.w.xc(d, o == 1)] + self.sib[i]

    def far_x(self):
        self.join(0)
        self.x.far(1)
        self.join(1, 2)
        self.x.near(1)
        self.join(3)
        self.x.far(0)

    def far_z(self):
        self.z.far(1)
        self.z.near(1)
        self.z.far(0)

    def to_y(self, j, dev, value):
        self.mid[j] = value
        self.posts.post(self.mid.at[j], self.ybuf.at[j], self.r_y.at[j], dev)

    def to_y_x(self):
        self.to_y(1, (self.w.r, self.w.xc(0, True)), self.x.total(1))

    def to_y_z(self):
        self.to_y(0, (self.w.zr(0, True), self.w.c), self.z.total(1))

    def own(self, j, ring):
        self.mid[2 + j] = ring.total(0)

    def final(self, j):
        self.posts.arrived(self.ybuf.at[j], self.r_y.at[j], self.sibling)
        return self.mid[2 + j] + self.ybuf[j]


RING_SCRATCH = [
    pltpu.VMEM((2, 2, HALF, NV), F32),
    pltpu.VMEM((2, 2, HALF, NV), F32),
    pltpu.VMEM((2, 2, GROUP, NV), F32),
    pltpu.SemaphoreType.DMA((2,)),
    pltpu.SemaphoreType.DMA((2,)),
]
RS_SCRATCH = (
    [
        pltpu.VMEM((8, GROUP, NV), F32),
        pltpu.VMEM((8, GROUP, NV), F32),
        pltpu.SemaphoreType.DMA((8,)),
    ]
    + RING_SCRATCH
    + RING_SCRATCH
    + [
        pltpu.VMEM((4, GROUP, NV), F32),
        pltpu.VMEM((2, GROUP, NV), F32),
        pltpu.SemaphoreType.DMA((2,)),
    ]
)
POOLS = [pltpu.SemaphoreType.DMA((n,)) for n in (34, 22, 34)]


class GramSum:
    def __init__(self, w, full, part, g1, s1, g2, s2, send, recv):
        self.w, self.full, self.part = w, full, part
        self.g1, self.s1, self.g2, self.s2 = g1, s1, g2, s2
        self.send, self.recv = send, recv

    def over_col(self, i, src, dst):
        w = self.w
        for d in (8, 7, 9, 6, 10, 5, 11, 4, 12, 3, 13, 2, 14, 1, 15):
            to = (w.c + d) % NCOL
            rcopy(src(to), dst.at[w.c], self.send.at[i], self.recv.at[i], (w.r, to)).start()

    def over_row(self, i, src, dst):
        w = self.w
        for d in (4, 3, 5, 2, 6, 1, 7):
            to = (w.r + d) % NROW
            rcopy(src, dst.at[w.r], self.send.at[i], self.recv.at[i], (to, w.c)).start()

    def all_of(self, i, ref, count):
        part = ref.at[pl.ds(0, count - 1)]
        return rcopy(part, part, self.send.at[i], self.recv.at[i], (self.w.r, self.w.xc(1)))

    def phase1(self):
        w = self.w
        self.over_col(0, lambda to: self.part.at[to], self.g1)
        self.g1[w.c] = self.part[w.c]

    def phase2(self):
        w = self.w
        self.all_of(0, self.g1, NCOL).wait_recv()
        total = self.g1[0]
        for i in range(1, NCOL):
            total = total + self.g1[i]
        self.s1[...] = total
        self.over_row(1, self.s1, self.g2)
        self.g2[w.r] = total

    def phase3(self):
        w = self.w
        self.all_of(1, self.g2, NROW).wait_recv()
        total = self.g2[0]
        for i in range(1, NROW):
            total = total + self.g2[i]
        total = total * (1.0 / (2 * GROUP * NROW * NCOL))
        self.s2[...] = total
        self.over_col(2, lambda to: self.s2, self.full)
        self.full[w.c] = total

    def join(self):
        self.all_of(2, self.full, NCOL).wait_recv()

    def drain(self):
        for i, ref in enumerate((self.g1, self.g2, self.full)):
            self.all_of(i, ref, NROW if i == 1 else NCOL).wait_send()


GRAM_SCRATCH = [
    pltpu.VMEM((NCOL, 8, NV), F32),
    pltpu.VMEM((NCOL, 8, NV), F32),
    pltpu.VMEM((8, NV), F32),
    pltpu.VMEM((NROW, 8, NV), F32),
    pltpu.VMEM((8, NV), F32),
    pltpu.SemaphoreType.DMA((3,)),
    pltpu.SemaphoreType.DMA((3,)),
]
NG = len(GRAM_SCRATCH)
NR = len(RS_SCRATCH)


def self_product(v):
    return lax.dot_general(v, v, (((0,), (0,)), ((), ())), precision=HIGH, preferred_element_type=F32)


def times_inverse(v, linv):
    return lax.dot_general(v, linv, (((1,), (1,)), ((), ())), precision=HIGH, preferred_element_type=F32)


def eliminate(gram, first, last):
    lane = lax.broadcasted_iota(jnp.int32, (8, NV), 1)
    sub = lax.broadcasted_iota(jnp.int32, (8, NV), 0)
    row = lax.broadcasted_iota(jnp.int32, (NV, NV), 0)
    inside = lax.broadcasted_iota(jnp.int32, (NV, NV), 1) < 8
    def block(it, w):
        top = w[:8]
        cols = [jnp.broadcast_to(w[:, i:i+1], (NV, NV)) for i in range(8)]
        b = [c[:8] for c in cols]
        x = jnp.where(lane < 8, jnp.where(lane == sub, 1.0, 0.0), top)
        fin = x
        for j in range(8):
            here = sub == j
            p = jnp.broadcast_to(b[j][j:j+1], (8, NV))
            inv = 1.0 / p
            xr = jnp.broadcast_to(x[j:j+1], (8, NV))
            fin = jnp.where(here, xr * (1.0 / jnp.sqrt(p)), fin)
            xs = xr * inv
            cj = b[j]
            x = jnp.where(here, xs, x - cj * xs)
            for k in range(j + 1, 8):
                bs = jnp.broadcast_to(b[k][j:j+1], (8, NV)) * inv
                b[k] = jnp.where(here, bs, b[k] - cj * bs)
        upd = jnp.where(inside, 0.0, w)
        for i in range(8):
            upd = upd - cols[i] * jnp.broadcast_to(x[i:i+1], (NV, NV))
        w = jnp.where(row < NV - 8 * it, upd, w)
        w = jnp.concatenate([w[8:], fin], axis=0)
        return pltpu.roll(w, NV - 8, 1)
    return lax.fori_loop(first, last, block, gram)


def lower_part(w):
    row = lax.broadcasted_iota(jnp.int32, (NV, NV), 0)
    return jnp.where(lax.broadcasted_iota(jnp.int32, (NV, NV), 1) <= row, w, 0.0)


def split(v):
    hi = v.astype(BF16)
    lo = (v - hi.astype(F32)).astype(BF16)
    return hi, lo


def link_tables(coords, links, ends):
    listed = coords.shape[1]
    lane = lax.broadcasted_iota(jnp.int32, (listed, listed), 1)
    sub = lax.broadcasted_iota(jnp.int32, (listed, listed), 0)
    count = lax.broadcasted_iota(jnp.int32, (listed, NV), 0) + 1
    place = lax.broadcasted_iota(jnp.int32, (listed, NV), 1)
    links[...] = jnp.zeros(links.shape, jnp.int32)
    ends[...] = jnp.zeros(ends.shape, jnp.int32)
    for t in (0, 1):
        along = jnp.broadcast_to(coords[t : t + 1, :], (listed, listed))
        down = jnp.max(jnp.where(lane == sub, along, 0), axis=1, keepdims=True)
        before = jnp.logical_and(jnp.broadcast_to(down, (listed, listed)) == along, sub < lane)
        links[t : t + 1, :listed] = jnp.max(jnp.where(before, sub + 1, 0), axis=0, keepdims=True)
        here = jnp.broadcast_to(down, (listed, NV)) == place
        ends[t : t + 1, :] = jnp.max(jnp.where(here, count, 0), axis=0, keepdims=True)


class Tile:
    def __init__(self, places, links, ends, blocks, sem, flat, chain, wcol, xrow):
        self.places, self.links, self.ends, self.blocks, self.sem = places, links, ends, blocks, sem
        self.flat, self.chain, self.wcol, self.xrow = flat, chain, wcol, xrow
        self.steps = blocks.shape[0] // CHUNK

    def piece(self, i):
        return pltpu.make_async_copy(
            self.blocks.at[pl.ds(i * CHUNK, CHUNK)],
            self.chain.at[pl.ds(i * CHUNK + 1, CHUNK)],
            self.sem.at[i],
        )

    def fetch(self):
        for i in range(self.steps):
            self.piece(i).start()

    def convert(self, lo, hi):
        for i in range(lo, hi):
            self.piece(i).wait()

            def one(k, carry):
                hi_part, lo_part = split(self.chain[i * CHUNK + 1 + k])
                self.flat[i * CHUNK + k] = jnp.concatenate([hi_part, lo_part], axis=1)
                return carry

            lax.fori_loop(0, CHUNK, one, 0, unroll=CHUNK)

    def clear(self):
        self.chain[0] = jnp.zeros((BLK, BLK), F32)

    def take_cols(self, colbuf):
        def one(i, carry):
            hi, lo = split(colbuf[i])
            for h in (0, 1):
                a, b = hi[h * BLK : (h + 1) * BLK], lo[h * BLK : (h + 1) * BLK]
                self.wcol[2 * i + h] = jnp.concatenate([jnp.concatenate([a, b], axis=1)] * 2, axis=0)
            return carry

        lax.fori_loop(0, NROW, one, 0, unroll=4)

    def take_rows(self, rowbuf):
        def one(i, carry):
            hi, lo = split(rowbuf[i].T)
            for h in (0, 1):
                a, b = hi[:, h * BLK : (h + 1) * BLK], lo[:, h * BLK : (h + 1) * BLK]
                self.xrow[2 * i + h] = jnp.concatenate([a, b], axis=1)
            return carry

        lax.fori_loop(0, NCOL, one, 0, unroll=4)

    def direct(self, lo, hi):
        def step(i, carry):
            for b in range(CHUNK):
                k = i * CHUNK + b
                d = jnp.dot(self.flat[k], self.wcol[self.places[1, k]], preferred_element_type=F32)
                self.chain[k + 1] = d[:, :NV] + d[:, NV:] + self.chain[self.links[0, k]]
            return carry

        lax.fori_loop(lo, hi, step, 0)

    def summed(self, rows):
        def out(i, carry):
            for h in (0, 1):
                rows[i, pl.ds(h * BLK, BLK)] = self.chain[self.ends[0, 2 * i + h]]
            return carry

        lax.fori_loop(0, NCOL, out, 0, unroll=4)

    def flip(self, lo, hi):
        def step(i, carry):
            for b in range(CHUNK):
                k = i * CHUNK + b
                flat = self.flat[k]
                e = jnp.dot(
                    self.xrow[self.places[0, k]],
                    jnp.concatenate([flat, flat], axis=0),
                    preferred_element_type=F32,
                )
                self.chain[k + 1] = e[:, :BLK] + e[:, BLK:] + self.chain[self.links[1, k]]
            return carry

        lax.fori_loop(lo, hi, step, 0)

    def flipped(self, cols):
        def out(i, carry):
            for h in (0, 1):
                cols[i, pl.ds(h * BLK, BLK)] = self.chain[self.ends[1, 2 * i + h]].T
            return carry

        lax.fori_loop(0, NROW, out, 0, unroll=4)


APP_SCRATCH = (
    [pltpu.VMEM((NCOL, GROUP, NV), F32), pltpu.VMEM((NROW, GROUP, NV), F32)]
    + GATHER_SEMS
    + RS_SCRATCH
    + [pltpu.VMEM((NCOL, 8, NV), F32)]
    + GRAM_SCRATCH
)
NA = len(APP_SCRATCH)


def whole_kernel(
    places, coords, blocks, vec, out, links, ends, vlinks, vends, s_tab, sem, flat, chain, wcol, xrow, rows, cols, pool1, pool2, pool3, work, *scratch
):
    w = Where()
    tile = Tile(places, links, ends, blocks, sem, flat, chain, wcol, xrow)
    n = tile.steps
    tile.fetch()
    entry_barrier(w.neighbours())
    posts1, posts2, posts3 = Posts(pool1), Posts(pool2), Posts(pool3)

    class App:
        def __init__(self, refs, up, lo, gather_posts, scatter_posts):
            self.rowbuf, self.colbuf = refs[:2]
            at = 2 + NS
            self.full = refs[at + NR]
            self.part = refs[at + NR + 1]
            self.g = Gather(w, gather_posts, up, lo, self.rowbuf, self.colbuf, *refs[2:at])
            self.s = Scatter(w, scatter_posts, rows, cols, refs[at : at + NR])
            self.gram = GramSum(w, self.full, *refs[at + NR + 1 :])

    one = App(scratch[:NA], vec.at[0], vec.at[1], posts1, posts1)
    two = App(scratch[NA : 2 * NA], out.at[0], out.at[1], posts2, posts3)

    g, s = one.g, one.s
    g.start_y_l()
    g.start_y_u()
    g.start_l()
    g.start_u()
    link_tables(coords, vlinks, vends)
    tables = [
        pltpu.make_async_copy(vlinks, links, s_tab.at[0]),
        pltpu.make_async_copy(vends, ends, s_tab.at[1]),
    ]
    for t in tables:
        t.start()
    tile.clear()
    tile.convert(0, 3)
    g.from_y_l()
    g.from_y_u()
    tile.convert(3, 6)
    g.from_x(False)
    tile.convert(6, n)
    for t in tables:
        t.wait()
    g.rest_l()
    tile.take_cols(one.colbuf)
    tile.direct(0, 3)
    g.from_x(True, (1,))
    tile.direct(3, 6)
    g.from_x(True, (3, 2))
    tile.direct(6, n)
    tile.summed(rows)
    s.siblings()
    g.rest_u()
    tile.take_rows(one.rowbuf)
    tile.flip(0, 3)
    s.far_x()
    s.join(4, 5)
    tile.flip(3, n)
    tile.flipped(cols)
    s.far_z()
    s.x.through(1)
    s.x.near(0)
    s.join(6, 7)
    s.x.through(0)
    s.to_y_x()
    s.z.through(1)
    s.z.near(0)
    s.z.through(0)
    s.own(1, s.x)
    out[0] = s.final(1) * LIFT
    g = two.g
    g.start_y_u()
    g.start_u()
    s.to_y_z()
    part = self_product(out[0])
    s.own(0, s.z)
    out[1] = s.final(0) * LIFT
    g.start_y_l()
    g.start_l()
    one.part[...] = (part + self_product(out[1])).reshape(NCOL, 8, NV)
    one.gram.phase1()

    s = two.s
    g.from_y_u()
    g.from_x(False)
    g.from_y_l()
    g.from_x(True)
    one.gram.phase2()
    g.rest_u()
    tile.take_rows(two.rowbuf)
    tile.flip(0, n)
    posts1.drain()
    tile.flipped(cols)
    s.far_z()
    one.gram.phase3()
    g.rest_l()
    tile.take_cols(two.colbuf)
    tile.direct(0, n)
    tile.summed(rows)
    s.siblings()
    s.z.through(1)
    s.z.near(0)
    s.far_x()
    s.z.through(0)
    s.join(4, 5)
    one.gram.join()
    one.gram.drain()
    work[...] = eliminate(one.full[...].reshape(NV, NV), 0, 4)
    s.x.through(1)
    s.x.near(0)
    s.join(6, 7)
    work[...] = eliminate(work[...], 4, 8)
    s.x.through(0)
    s.to_y_z()
    work[...] = eliminate(work[...], 8, 12)
    s.own(0, s.z)
    s.to_y_x()
    work[...] = lower_part(eliminate(work[...], 12, 16))
    posts2.drain()
    out[1] = times_inverse(s.final(0), work[...])
    part = self_product(out[1])
    s.own(1, s.x)
    out[0] = times_inverse(s.final(1), work[...])
    two.part[...] = (part + self_product(out[0])).reshape(NCOL, 8, NV)
    two.gram.phase1()
    two.gram.phase2()
    two.gram.phase3()
    two.gram.join()
    linv = lower_part(eliminate(two.full[...].reshape(NV, NV), 0, 16))
    two.gram.drain()
    posts3.drain()
    out[0] = times_inverse(out[0], linv)
    out[1] = times_inverse(out[1], linv)


def local(blocks, coords, vectors):
    values = blocks.reshape(blocks.shape[2], BLK, BLK)
    places = coords.reshape(2, coords.shape[3])
    listed = values.shape[0]
    scalars = pl.BlockSpec(memory_space=pltpu.SMEM)
    return pl.pallas_call(
        whole_kernel,
        out_shape=jax.ShapeDtypeStruct((2, GROUP, NV), F32),
        in_specs=[scalars, VM, pl.BlockSpec(memory_space=pl.ANY), VM],
        out_specs=VM,
        scratch_shapes=[
            pltpu.SMEM((8, 256), jnp.int32),
            pltpu.SMEM((8, NV), jnp.int32),
            pltpu.VMEM((8, 256), jnp.int32),
            pltpu.VMEM((8, NV), jnp.int32),
            pltpu.SemaphoreType.DMA((2,)),
            pltpu.SemaphoreType.DMA((listed // CHUNK,)),
            pltpu.VMEM((listed, BLK, 2 * BLK), BF16),
            pltpu.VMEM((listed + 1, BLK, BLK), F32),
            pltpu.VMEM((16, 2 * BLK, 2 * NV), BF16),
            pltpu.VMEM((32, NV, 2 * BLK), BF16),
            pltpu.VMEM((NCOL, GROUP, NV), F32),
            pltpu.VMEM((NROW, GROUP, NV), F32),
        ]
        + POOLS
        + [pltpu.VMEM((NV, NV), F32)]
        + APP_SCRATCH
        + APP_SCRATCH,
        compiler_params=pltpu.CompilerParams(
            collective_id=0, has_side_effects=True, vmem_limit_bytes=56 << 20
        ),
        name="whole",
    )(places, places, values, vectors)


def solution(mesh):
    return jax.shard_map(
        local,
        mesh=mesh,
        in_specs=(
            P("row", "col", None, None, None),
            P("row", "col", None, None),
            P(None, ("row", "col"), None),
        ),
        out_specs=P(None, ("row", "col"), None),
        check_vma=False,
    )
```

```python
import functools

import jax
import jax.numpy as jnp
from jax import lax
from jax.experimental import pallas as pl
from jax.experimental.pallas import tpu as pltpu
from jax.sharding import PartitionSpec as P

MESH = pl.DeviceIdType.MESH
HIGH = lax.Precision.HIGHEST
F32 = jnp.float32
BF16 = jnp.bfloat16

GROUP = 256
NV = 128
BLK = 128
NROW = 8
NCOL = 16
CHUNK = 17
VM = pl.BlockSpec(memory_space=pltpu.VMEM)
LIFT = 2.0**20


class Where:
    def __init__(self):
        self.r = lax.axis_index("row")
        self.c = lax.axis_index("col")
        self.z = self.r // 2
        self.yl = self.r % 2
        self.yh = self.c // 8
        self.x = (self.c // 2) % 4
        self.core = self.c % 2

    def zr(self, dz, other=False):
        yl = 1 - self.yl if other else self.yl
        return ((self.z + dz) % 4) * 2 + yl

    def xc(self, dx, other_y=False, other_core=False):
        yh = 1 - self.yh if other_y else self.yh
        core = 1 - self.core if other_core else self.core
        return (yh * 4 + (self.x + dx) % 4) * 2 + core

    def neighbours(self):
        out = [(self.zr(dz), self.c) for dz in (1, 2, 3)]
        out.append((self.zr(0, True), self.c))
        out += [(self.r, self.xc(dx)) for dx in (1, 2, 3)]
        out.append((self.r, self.xc(0, True)))
        out.append((self.r, self.xc(0, False, True)))
        return out


def entry_barrier(partners):
    barrier = pltpu.get_barrier_semaphore()
    for p in partners:
        pl.semaphore_signal(barrier, inc=1, device_id=p, device_id_type=MESH)
    pl.semaphore_wait(barrier, len(partners))


def rcopy(src, dst, send, recv, dev):
    return pltpu.make_async_remote_copy(
        src_ref=src,
        dst_ref=dst,
        send_sem=send,
        recv_sem=recv,
        device_id=dev,
        device_id_type=MESH,
    )


HALF = GROUP // 2


def half(ref, h):
    return ref.at[pl.ds(h * HALF, HALF)]


class Posts:
    def __init__(self, pool):
        self.pool = pool
        self.sent = []
        self.oldest = 0

    def post(self, src, dst, recv, dev):
        slots = self.pool.shape[0]
        if len(self.sent) - self.oldest == slots:
            self.sent[self.oldest].wait_send()
            self.oldest += 1
        cp = rcopy(src, dst, self.pool.at[len(self.sent) % slots], recv, dev)
        cp.start()
        self.sent.append(cp)
        return cp

    def arrived(self, ref, recv, dev):
        rcopy(ref, ref, self.pool.at[0], recv, dev).wait_recv()

    def drain(self):
        for cp in self.sent[self.oldest :]:
            cp.wait_send()
        self.oldest = len(self.sent)


class Gather:
    def __init__(self, w, posts, up, lo, rowbuf, colbuf, r_u, r_sib, r_y, r_l):
        self.w, self.posts, self.up, self.lo = w, posts, up, lo
        self.rowbuf, self.colbuf = rowbuf, colbuf
        self.r_u, self.r_sib, self.r_y, self.r_l = r_u, r_sib.at[0], r_y.at[0], r_l.at[0]
        self.sibling = (w.r, w.xc(0, False, True))

    def send_u(self, src, p, dev):
        self.posts.post(src, self.rowbuf.at[p], self.r_u.at[p // 2], dev)

    def to_sibling(self, src, p):
        self.posts.post(src, self.rowbuf.at[p], self.r_sib, self.sibling)

    def send_l(self, src, q, recv, dev):
        self.posts.post(src, self.colbuf.at[q], recv, dev)

    def wait_u(self, p):
        self.posts.arrived(self.rowbuf.at[p], self.r_u.at[p // 2], self.sibling)

    def start_y_l(self):
        self.send_l(self.lo, self.w.r, self.r_y, (self.w.zr(0, True), self.w.c))

    def start_y_u(self):
        self.send_u(self.up, self.w.c, (self.w.r, self.w.xc(0, True)))

    def start_l(self):
        w = self.w
        for d in (2, 1, 3):
            self.send_l(self.lo, w.r, self.r_l, (w.zr(d), w.c))
        self.colbuf[w.r] = self.lo[...]

    def start_u(self):
        w = self.w
        for d in (2, 1, 3):
            self.send_u(self.up, w.c, (w.r, w.xc(d)))
        self.to_sibling(self.up, w.c)
        self.rowbuf[w.c] = self.up[...]

    def from_y_l(self):
        w = self.w
        q = w.zr(0, True)
        self.posts.arrived(self.colbuf.at[q], self.r_y, self.sibling)
        for d in (2, 1, 3):
            self.send_l(self.colbuf.at[q], q, self.r_l, (w.zr(d), w.c))

    def from_y_u(self):
        w = self.w
        p = w.xc(0, True)
        self.wait_u(p)
        for d in (2, 1, 3):
            self.send_u(self.rowbuf.at[p], p, (w.r, w.xc(d)))
        self.to_sibling(self.rowbuf.at[p], p)

    def from_x(self, other, steps=(1, 3, 2)):
        for d in steps:
            p = self.w.xc(d, other)
            self.wait_u(p)
            self.to_sibling(self.rowbuf.at[p], p)

    def rest_l(self):
        self.posts.arrived(self.colbuf.at[pl.ds(0, 6)], self.r_l, self.sibling)

    def rest_u(self):
        self.posts.arrived(self.rowbuf.at[pl.ds(0, 8)], self.r_sib, self.sibling)


GATHER_SEMS = [pltpu.SemaphoreType.DMA((n,)) for n in (8, 1, 1, 1)]
NS = len(GATHER_SEMS)


class Ring:
    def __init__(self, posts, dev, part, dep, rel, fin, r_rel, r_fin):
        self.posts, self.dev, self.part = posts, dev, part
        self.dep, self.rel, self.fin = dep, rel, fin
        self.r_rel, self.r_fin = r_rel, r_fin

    def far(self, o):
        for k, s in enumerate((1, -1)):
            self.posts.post(half(self.part(2, o), k), self.rel.at[o, k], self.r_rel.at[o], self.dev(s))

    def near(self, o):
        for k, s in enumerate((1, -1)):
            h = 1 - k
            self.posts.post(half(self.part(s, o), h), half(self.fin.at[o, k], h), self.r_fin.at[o], self.dev(s))

    def through(self, o):
        self.posts.arrived(self.rel.at[o], self.r_rel.at[o], self.dev(1))
        for k, s in enumerate((1, -1)):
            self.dep[o, k] = half(self.part(s, o), k)[...] + self.rel[o, k]
            self.posts.post(self.dep.at[o, k], half(self.fin.at[o, k], k), self.r_fin.at[o], self.dev(s))

    def total(self, o):
        self.posts.arrived(self.fin.at[o], self.r_fin.at[o], self.dev(1))
        return self.part(0, o)[...] + self.fin[o, 0] + self.fin[o, 1]


class Scatter:
    SLOTS = [(2, 1), (1, 1), (3, 1), (2, 0), (1, 0), (3, 0), (0, 1), (0, 0)]

    def __init__(self, w, posts, rows, cols, scratch):
        self.acc, self.sib, self.r_sib = scratch[:3]
        x, z = scratch[3:8], scratch[8:13]
        self.mid, self.ybuf, self.r_y = scratch[13:]
        self.w, self.posts, self.rows = w, posts, rows
        self.sibling = (w.r, w.xc(0, False, True))
        at = {slot: i for i, slot in enumerate(self.SLOTS)}
        self.x = Ring(posts, lambda s: (w.r, w.xc(s % 4)), lambda d, o: self.acc.at[at[d % 4, o]], *x)
        self.z = Ring(posts, lambda s: (w.zr(s % 4), w.c), lambda d, o: cols.at[w.zr(d % 4, o == 1)], *z)

    def siblings(self):
        for i, (d, o) in enumerate(self.SLOTS):
            src = self.rows.at[self.w.xc(d, o == 1, True)]
            self.posts.post(src, self.sib.at[i], self.r_sib.at[i], self.sibling)

    def join(self, *ids):
        for i in ids:
            self.posts.arrived(self.sib.at[i], self.r_sib.at[i], self.sibling)
            d, o = self.SLOTS[i]
            self.acc[i] = self.rows[self.w.xc(d, o == 1)] + self.sib[i]

    def far_x(self):
        self.join(0)
        self.x.far(1)
        self.join(1, 2)
        self.x.near(1)
        self.join(3)
        self.x.far(0)

    def far_z(self):
        self.z.far(1)
        self.z.near(1)
        self.z.far(0)

    def to_y(self, j, dev, value):
        self.mid[j] = value
        self.posts.post(self.mid.at[j], self.ybuf.at[j], self.r_y.at[j], dev)

    def to_y_x(self):
        self.to_y(1, (self.w.r, self.w.xc(0, True)), self.x.total(1))

    def to_y_z(self):
        self.to_y(0, (self.w.zr(0, True), self.w.c), self.z.total(1))

    def own(self, j, ring):
        self.mid[2 + j] = ring.total(0)

    def final(self, j):
        self.posts.arrived(self.ybuf.at[j], self.r_y.at[j], self.sibling)
        return self.mid[2 + j] + self.ybuf[j]


RING_SCRATCH = [
    pltpu.VMEM((2, 2, HALF, NV), F32),
    pltpu.VMEM((2, 2, HALF, NV), F32),
    pltpu.VMEM((2, 2, GROUP, NV), F32),
    pltpu.SemaphoreType.DMA((2,)),
    pltpu.SemaphoreType.DMA((2,)),
]
RS_SCRATCH = (
    [
        pltpu.VMEM((8, GROUP, NV), F32),
        pltpu.VMEM((8, GROUP, NV), F32),
        pltpu.SemaphoreType.DMA((8,)),
    ]
    + RING_SCRATCH
    + RING_SCRATCH
    + [
        pltpu.VMEM((4, GROUP, NV), F32),
        pltpu.VMEM((2, GROUP, NV), F32),
        pltpu.SemaphoreType.DMA((2,)),
    ]
)
POOLS = [pltpu.SemaphoreType.DMA((n,)) for n in (34, 22, 34)]


class GramSum:
    def __init__(self, w, full, part, g1, s1, g2, s2, send, recv):
        self.w, self.full, self.part = w, full, part
        self.g1, self.s1, self.g2, self.s2 = g1, s1, g2, s2
        self.send, self.recv = send, recv

    def over_col(self, i, src, dst):
        w = self.w
        for d in (8, 7, 9, 6, 10, 5, 11, 4, 12, 3, 13, 2, 14, 1, 15):
            to = (w.c + d) % NCOL
            rcopy(src(to), dst.at[w.c], self.send.at[i], self.recv.at[i], (w.r, to)).start()

    def over_row(self, i, src, dst):
        w = self.w
        for d in (4, 3, 5, 2, 6, 1, 7):
            to = (w.r + d) % NROW
            rcopy(src, dst.at[w.r], self.send.at[i], self.recv.at[i], (to, w.c)).start()

    def all_of(self, i, ref, count):
        part = ref.at[pl.ds(0, count - 1)]
        return rcopy(part, part, self.send.at[i], self.recv.at[i], (self.w.r, self.w.xc(1)))

    def phase1(self):
        w = self.w
        self.over_col(0, lambda to: self.part.at[to], self.g1)
        self.g1[w.c] = self.part[w.c]

    def phase2(self):
        w = self.w
        self.all_of(0, self.g1, NCOL).wait_recv()
        total = self.g1[0]
        for i in range(1, NCOL):
            total = total + self.g1[i]
        self.s1[...] = total
        self.over_row(1, self.s1, self.g2)
        self.g2[w.r] = total

    def phase3(self):
        w = self.w
        self.all_of(1, self.g2, NROW).wait_recv()
        total = self.g2[0]
        for i in range(1, NROW):
            total = total + self.g2[i]
        total = total * (1.0 / (2 * GROUP * NROW * NCOL))
        self.s2[...] = total
        self.over_col(2, lambda to: self.s2, self.full)
        self.full[w.c] = total

    def join(self):
        self.all_of(2, self.full, NCOL).wait_recv()

    def drain(self):
        for i, ref in enumerate((self.g1, self.g2, self.full)):
            self.all_of(i, ref, NROW if i == 1 else NCOL).wait_send()


GRAM_SCRATCH = [
    pltpu.VMEM((NCOL, 8, NV), F32),
    pltpu.VMEM((NCOL, 8, NV), F32),
    pltpu.VMEM((8, NV), F32),
    pltpu.VMEM((NROW, 8, NV), F32),
    pltpu.VMEM((8, NV), F32),
    pltpu.SemaphoreType.DMA((3,)),
    pltpu.SemaphoreType.DMA((3,)),
]
NG = len(GRAM_SCRATCH)
NR = len(RS_SCRATCH)


def self_product(v):
    return lax.dot_general(v, v, (((0,), (0,)), ((), ())), precision=HIGH, preferred_element_type=F32)


def times_inverse(v, linv):
    return lax.dot_general(v, linv, (((1,), (1,)), ((), ())), precision=HIGH, preferred_element_type=F32)


def eliminate(gram, first, last):
    lane = lax.broadcasted_iota(jnp.int32, (8, NV), 1)
    sub = lax.broadcasted_iota(jnp.int32, (8, NV), 0)
    row = lax.broadcasted_iota(jnp.int32, (NV, NV), 0)
    inside = lax.broadcasted_iota(jnp.int32, (NV, NV), 1) < 8
    def block(it, w):
        top = w[:8]
        cols = [jnp.broadcast_to(w[:, i:i+1], (NV, NV)) for i in range(8)]
        b = [c[:8] for c in cols]
        x = jnp.where(lane < 8, jnp.where(lane == sub, 1.0, 0.0), top)
        fin = x
        for j in range(8):
            here = sub == j
            p = jnp.broadcast_to(b[j][j:j+1], (8, NV))
            inv = 1.0 / p
            xr = jnp.broadcast_to(x[j:j+1], (8, NV))
            fin = jnp.where(here, xr * (1.0 / jnp.sqrt(p)), fin)
            xs = xr * inv
            cj = b[j]
            x = jnp.where(here, xs, x - cj * xs)
            for k in range(j + 1, 8):
                bs = jnp.broadcast_to(b[k][j:j+1], (8, NV)) * inv
                b[k] = jnp.where(here, bs, b[k] - cj * bs)
        upd = jnp.where(inside, 0.0, w)
        for i in range(8):
            upd = upd - cols[i] * jnp.broadcast_to(x[i:i+1], (NV, NV))
        w = jnp.where(row < NV - 8 * it, upd, w)
        w = jnp.concatenate([w[8:], fin], axis=0)
        return pltpu.roll(w, NV - 8, 1)
    return lax.fori_loop(first, last, block, gram)


def lower_part(w):
    row = lax.broadcasted_iota(jnp.int32, (NV, NV), 0)
    return jnp.where(lax.broadcasted_iota(jnp.int32, (NV, NV), 1) <= row, w, 0.0)


def split(v):
    hi = v.astype(BF16)
    lo = (v - hi.astype(F32)).astype(BF16)
    return hi, lo


def link_tables(coords, links, ends):
    listed = coords.shape[1]
    lane = lax.broadcasted_iota(jnp.int32, (listed, listed), 1)
    sub = lax.broadcasted_iota(jnp.int32, (listed, listed), 0)
    count = lax.broadcasted_iota(jnp.int32, (listed, NV), 0) + 1
    place = lax.broadcasted_iota(jnp.int32, (listed, NV), 1)
    links[...] = jnp.zeros(links.shape, jnp.int32)
    ends[...] = jnp.zeros(ends.shape, jnp.int32)
    for t in (0, 1):
        along = jnp.broadcast_to(coords[t : t + 1, :], (listed, listed))
        down = jnp.max(jnp.where(lane == sub, along, 0), axis=1, keepdims=True)
        before = jnp.logical_and(jnp.broadcast_to(down, (listed, listed)) == along, sub < lane)
        links[t : t + 1, :listed] = jnp.max(jnp.where(before, sub + 1, 0), axis=0, keepdims=True)
        here = jnp.broadcast_to(down, (listed, NV)) == place
        ends[t : t + 1, :] = jnp.max(jnp.where(here, count, 0), axis=0, keepdims=True)


class Tile:
    def __init__(self, places, links, ends, blocks, sem, flat, chain, wcol, xrow):
        self.places, self.links, self.ends, self.blocks, self.sem = places, links, ends, blocks, sem
        self.flat, self.chain, self.wcol, self.xrow = flat, chain, wcol, xrow
        self.steps = blocks.shape[0] // CHUNK

    def piece(self, i):
        return pltpu.make_async_copy(
            self.blocks.at[pl.ds(i * CHUNK, CHUNK)],
            self.chain.at[pl.ds(i * CHUNK + 1, CHUNK)],
            self.sem.at[i],
        )

    def fetch(self):
        for i in range(self.steps):
            self.piece(i).start()

    def convert(self, lo, hi):
        for i in range(lo, hi):
            self.piece(i).wait()

            def one(k, carry):
                hi_part, lo_part = split(self.chain[i * CHUNK + 1 + k])
                self.flat[i * CHUNK + k] = jnp.concatenate([hi_part, lo_part], axis=1)
                return carry

            lax.fori_loop(0, CHUNK, one, 0, unroll=CHUNK)

    def clear(self):
        self.chain[0] = jnp.zeros((BLK, BLK), F32)

    def take_cols(self, colbuf):
        def one(i, carry):
            hi, lo = split(colbuf[i])
            for h in (0, 1):
                a, b = hi[h * BLK : (h + 1) * BLK], lo[h * BLK : (h + 1) * BLK]
                self.wcol[2 * i + h] = jnp.concatenate([jnp.concatenate([a, b], axis=1)] * 2, axis=0)
            return carry

        lax.fori_loop(0, NROW, one, 0, unroll=4)

    def take_rows(self, rowbuf):
        def one(i, carry):
            hi, lo = split(rowbuf[i].T)
            for h in (0, 1):
                a, b = hi[:, h * BLK : (h + 1) * BLK], lo[:, h * BLK : (h + 1) * BLK]
                self.xrow[2 * i + h] = jnp.concatenate([a, b], axis=1)
            return carry

        lax.fori_loop(0, NCOL, one, 0, unroll=4)

    def direct(self, lo, hi):
        def step(i, carry):
            for b in range(CHUNK):
                k = i * CHUNK + b
                d = jnp.dot(self.flat[k], self.wcol[self.places[1, k]], preferred_element_type=F32)
                self.chain[k + 1] = d[:, :NV] + d[:, NV:] + self.chain[self.links[0, k]]
            return carry

        lax.fori_loop(lo, hi, step, 0)

    def summed(self, rows):
        def out(i, carry):
            for h in (0, 1):
                rows[i, pl.ds(h * BLK, BLK)] = self.chain[self.ends[0, 2 * i + h]]
            return carry

        lax.fori_loop(0, NCOL, out, 0, unroll=4)

    def flip(self, lo, hi):
        def step(i, carry):
            for b in range(CHUNK):
                k = i * CHUNK + b
                flat = self.flat[k]
                e = jnp.dot(
                    self.xrow[self.places[0, k]],
                    jnp.concatenate([flat, flat], axis=0),
                    preferred_element_type=F32,
                )
                self.chain[k + 1] = e[:, :BLK] + e[:, BLK:] + self.chain[self.links[1, k]]
            return carry

        lax.fori_loop(lo, hi, step, 0)

    def flipped(self, cols):
        def out(i, carry):
            for h in (0, 1):
                cols[i, pl.ds(h * BLK, BLK)] = self.chain[self.ends[1, 2 * i + h]].T
            return carry

        lax.fori_loop(0, NROW, out, 0, unroll=4)


APP_SCRATCH = (
    [pltpu.VMEM((NCOL, GROUP, NV), F32), pltpu.VMEM((NROW, GROUP, NV), F32)]
    + GATHER_SEMS
    + RS_SCRATCH
    + [pltpu.VMEM((NCOL, 8, NV), F32)]
    + GRAM_SCRATCH
)
NA = len(APP_SCRATCH)


def whole_kernel(
    places, coords, blocks, vec, out, links, ends, vlinks, vends, s_tab, sem, flat, chain, wcol, xrow, rows, cols, pool1, pool2, pool3, work, *scratch
):
    w = Where()
    tile = Tile(places, links, ends, blocks, sem, flat, chain, wcol, xrow)
    n = tile.steps
    tile.fetch()
    entry_barrier(w.neighbours())
    posts1, posts2, posts3 = Posts(pool1), Posts(pool2), Posts(pool3)

    class App:
        def __init__(self, refs, up, lo, gather_posts, scatter_posts):
            self.rowbuf, self.colbuf = refs[:2]
            at = 2 + NS
            self.full = refs[at + NR]
            self.part = refs[at + NR + 1]
            self.g = Gather(w, gather_posts, up, lo, self.rowbuf, self.colbuf, *refs[2:at])
            self.s = Scatter(w, scatter_posts, rows, cols, refs[at : at + NR])
            self.gram = GramSum(w, self.full, *refs[at + NR + 1 :])

    one = App(scratch[:NA], vec.at[0], vec.at[1], posts1, posts1)
    two = App(scratch[NA : 2 * NA], out.at[0], out.at[1], posts2, posts3)

    g, s = one.g, one.s
    g.start_y_l()
    g.start_y_u()
    g.start_l()
    g.start_u()
    link_tables(coords, vlinks, vends)
    tables = [
        pltpu.make_async_copy(vlinks, links, s_tab.at[0]),
        pltpu.make_async_copy(vends, ends, s_tab.at[1]),
    ]
    for t in tables:
        t.start()
    tile.clear()
    tile.convert(0, 3)
    g.from_y_l()
    g.from_y_u()
    tile.convert(3, 6)
    g.from_x(False)
    tile.convert(6, n)
    for t in tables:
        t.wait()
    g.rest_l()
    tile.take_cols(one.colbuf)
    tile.direct(0, 3)
    g.from_x(True, (1,))
    tile.direct(3, 6)
    g.from_x(True, (3, 2))
    tile.direct(6, n)
    tile.summed(rows)
    s.siblings()
    g.rest_u()
    tile.take_rows(one.rowbuf)
    tile.flip(0, 3)
    s.far_x()
    s.join(4, 5)
    tile.flip(3, n)
    tile.flipped(cols)
    s.far_z()
    s.x.through(1)
    s.x.near(0)
    s.join(6, 7)
    s.x.through(0)
    s.z.through(1)
    s.z.near(0)
    s.to_y_x()
    s.z.through(0)
    s.own(1, s.x)
    out[0] = s.final(1) * LIFT
    g = two.g
    g.start_y_u()
    g.start_u()
    s.to_y_z()
    part = self_product(out[0])
    s.own(0, s.z)
    out[1] = s.final(0) * LIFT
    g.start_y_l()
    g.start_l()
    one.part[...] = (part + self_product(out[1])).reshape(NCOL, 8, NV)
    one.gram.phase1()

    s = two.s
    g.from_y_u()
    g.from_x(False)
    g.from_y_l()
    g.from_x(True)
    one.gram.phase2()
    g.rest_u()
    tile.take_rows(two.rowbuf)
    tile.flip(0, n)
    posts1.drain()
    tile.flipped(cols)
    s.far_z()
    one.gram.phase3()
    g.rest_l()
    tile.take_cols(two.colbuf)
    tile.direct(0, n)
    tile.summed(rows)
    s.siblings()
    s.z.through(1)
    s.z.near(0)
    s.far_x()
    s.z.through(0)
    s.join(4, 5)
    one.gram.join()
    one.gram.drain()
    work[...] = eliminate(one.full[...].reshape(NV, NV), 0, 4)
    s.x.through(1)
    s.x.near(0)
    s.join(6, 7)
    work[...] = eliminate(work[...], 4, 8)
    s.x.through(0)
    s.to_y_z()
    work[...] = eliminate(work[...], 8, 12)
    s.own(0, s.z)
    s.to_y_x()
    work[...] = lower_part(eliminate(work[...], 12, 16))
    posts2.drain()
    out[1] = times_inverse(s.final(0), work[...])
    part = self_product(out[1])
    s.own(1, s.x)
    out[0] = times_inverse(s.final(1), work[...])
    two.part[...] = (part + self_product(out[0])).reshape(NCOL, 8, NV)
    two.gram.phase1()
    two.gram.phase2()
    two.gram.phase3()
    two.gram.join()
    linv = lower_part(eliminate(two.full[...].reshape(NV, NV), 0, 16))
    two.gram.drain()
    posts3.drain()
    out[0] = times_inverse(out[0], linv)
    out[1] = times_inverse(out[1], linv)


def local(blocks, coords, vectors):
    values = blocks.reshape(blocks.shape[2], BLK, BLK)
    places = coords.reshape(2, coords.shape[3])
    listed = values.shape[0]
    scalars = pl.BlockSpec(memory_space=pltpu.SMEM)
    return pl.pallas_call(
        whole_kernel,
        out_shape=jax.ShapeDtypeStruct((2, GROUP, NV), F32),
        in_specs=[scalars, VM, pl.BlockSpec(memory_space=pl.ANY), VM],
        out_specs=VM,
        scratch_shapes=[
            pltpu.SMEM((8, 256), jnp.int32),
            pltpu.SMEM((8, NV), jnp.int32),
            pltpu.VMEM((8, 256), jnp.int32),
            pltpu.VMEM((8, NV), jnp.int32),
            pltpu.SemaphoreType.DMA((2,)),
            pltpu.SemaphoreType.DMA((listed // CHUNK,)),
            pltpu.VMEM((listed, BLK, 2 * BLK), BF16),
            pltpu.VMEM((listed + 1, BLK, BLK), F32),
            pltpu.VMEM((16, 2 * BLK, 2 * NV), BF16),
            pltpu.VMEM((32, NV, 2 * BLK), BF16),
            pltpu.VMEM((NCOL, GROUP, NV), F32),
            pltpu.VMEM((NROW, GROUP, NV), F32),
        ]
        + POOLS
        + [pltpu.VMEM((NV, NV), F32)]
        + APP_SCRATCH
        + APP_SCRATCH,
        compiler_params=pltpu.CompilerParams(
            collective_id=0, has_side_effects=True, vmem_limit_bytes=56 << 20
        ),
        name="whole",
    )(places, places, values, vectors)


def solution(mesh):
    return jax.shard_map(
        local,
        mesh=mesh,
        in_specs=(
            P("row", "col", None, None, None),
            P("row", "col", None, None),
            P(None, ("row", "col"), None),
        ),
        out_specs=P(None, ("row", "col"), None),
        check_vma=False,
    )
```
